512 devices in a mesh: seq: 128 (over x, z, core), batch: 4 (over y).
Axes of the slice: x: 4, y: 4, z: 16, core: 2. Of those that a mesh axis runs over, the one named last changes fastest.
Arguments:
- dna_bases: int32 [131072], P(('batch', 'seq')), parts along dimension 0, may hold values from 0 to 3
- stem_weight: bfloat16 [5, 4, 384], replicated, may hold values from -8 to 8
- stem_bias: float32 [384], replicated, may hold values from -4 to 0
- conv_weight: bfloat16 [5, 384, 768], replicated, may hold values from -0.4375 to 0.4375
- conv_bias: float32 [768], replicated, may hold values from -4 to 0
- norm_gain: float32 [768], replicated, may hold values from 0.25 to 1.75
- query_weight: bfloat16 [768, 1024], replicated, may hold values from -0.875 to 0.875
- key_weight: bfloat16 [768, 128], replicated, may hold values from -0.21875 to 0.21875
- value_weight: bfloat16 [768, 192], replicated, may hold values from -0.4375 to 0.4375
Outputs:
- attended: bfloat16 [32768, 1536], P(('batch', 'seq')), parts along dimension 0
The draws below stay inside these ranges and needn't reach their ends.
There are 4 independent parts, one for each index of `batch`. The reference program is written for one: setup_inputs(seed, part) draws one part's arguments, and reference() takes and returns one part's arrays. A program takes and returns all parts, laid end to end along the dimension named above; an argument that names none is the same for every part. Nothing has to cross between parts.
Inputs may be any that keep to these rules, and one draw needn't show every extreme that they name: `dna_bases`: codes for A, C, G and T in this order.
All inputs are finite; a program needn't handle non-finite values.
Results may differ from the reference program's by a relative error of at most 0.005.
Values may be sent and summed in bfloat16 or wider, within the bound.
A program may use at most 64 MiB of HBM per device.

```python
import math
import jax
import jax.numpy as jnp
from jax import lax

C1 = 384
C2 = 768
HEADS = 8
KD = 128
VD = 192
TAPS = 5
TOKENS = 8192
BASES = 32768


def set_ends(entries, own_key, least, high):
    dims = entries.shape
    spot = [jax.random.randint(jax.random.fold_in(own_key, axis), (), 0, dims[axis]) for axis in range(len(dims))]
    entries = entries.at[tuple(spot)].set(least)
    longest = dims.index(max(dims))
    spot[longest] = (spot[longest] + 1) % dims[longest]
    return entries.at[tuple(spot)].set(high)


def gaussian(key, shape, spread, bound, kind=jnp.bfloat16):
    entries = spread * jax.random.normal(key, shape, jnp.float32)
    return jnp.clip(entries, min=-bound, max=bound).astype(kind)


def setup_inputs(seed: int = 0, part: int = 0) -> dict:
    key_list = jax.random.split(jax.random.key(seed), 10)
    part_keys = jax.random.split(jax.random.fold_in(key_list[9], part), 10)
    dna_bases = set_ends(jax.random.randint(part_keys[0], (BASES,), 0, 4), jax.random.fold_in(part_keys[0], 1), 0, 3).astype(jnp.int32)
    stem_weight = gaussian(key_list[1], (TAPS, 4, C1), 1.35, 8.0)
    stem_bias = jnp.clip(jax.random.uniform(key_list[2], (C1,), jnp.float32, -4.0, 0.0), -4.0, 0.0)
    conv_weight = gaussian(key_list[3], (TAPS, C1, C2), (TAPS * C1 // 9) ** -0.5, 0.4375)
    conv_bias = jnp.clip(jax.random.uniform(key_list[4], (C2,), jnp.float32, -4.0, 0.0), -4.0, 0.0)
    norm_gain = jnp.clip(1.0 + 0.15 * jax.random.normal(key_list[5], (C2,), jnp.float32), 0.25, 1.75)
    query_weight = gaussian(key_list[6], (C2, HEADS * KD), (C2 // 16) ** -0.5, 0.875)
    key_weight = gaussian(key_list[7], (C2, KD), C2 ** -0.5, 0.21875)
    value_weight = gaussian(key_list[8], (C2, VD), (C2 // 4) ** -0.5, 0.4375)
    return {"dna_bases": dna_bases, "stem_weight": stem_weight, "stem_bias": stem_bias, "conv_weight": conv_weight, "conv_bias": conv_bias, "norm_gain": norm_gain, "query_weight": query_weight, "key_weight": key_weight, "value_weight": value_weight}


soft_cap = 20.0
rope_base = 10000.0

def encode(base_marks):
    return (base_marks[:, None] == jnp.arange(1, 5, dtype=jnp.int32)[None, :]).astype(jnp.bfloat16)

def shifted_sum(inputs, weight, shift_bias):
    out_rows = inputs.shape[0] - weight.shape[0] + 1
    summed = jnp.zeros((out_rows, weight.shape[2]), jnp.float32) + shift_bias[None, :]
    for offset in range(weight.shape[0]):
        summed = summed + jnp.dot(inputs[offset:offset + out_rows], weight[offset], preferred_element_type=jnp.float32)
    return summed

def gelu_pool(values_in):
    activated = jax.nn.gelu(values_in, approximate=True)
    return activated.reshape(values_in.shape[0] // 2, 2, values_in.shape[1]).max(axis=1)

def normalize(features, norm_gain):
    mean_square = lax.optimization_barrier(jnp.mean(features * features, axis=1, keepdims=True))
    return (features * lax.rsqrt(mean_square + 1e-06) * norm_gain[None, :]).astype(jnp.bfloat16)

def rotate(vectors, places):
    half_size = vectors.shape[-1] // 2
    frequency = jnp.exp(jnp.arange(half_size, dtype=jnp.float32) * (-2.0 * math.log(rope_base) / vectors.shape[-1]))
    angles = places.astype(jnp.float32)[:, None] * frequency[None, :]
    cosine = jnp.cos(angles)[:, None, :]
    sine_part = jnp.sin(angles)[:, None, :]
    first_half = vectors[..., :half_size]
    second_half = vectors[..., half_size:]
    return jnp.concatenate([first_half * cosine - second_half * sine_part, second_half * cosine + first_half * sine_part], axis=-1)

def reference(dna_bases, stem_weight, stem_bias, conv_weight, conv_bias, norm_gain, query_weight, key_weight, value_weight):
    reach_rows = TAPS // 2
    base_marks = jnp.pad(dna_bases + 1, reach_rows)
    pooled = gelu_pool(shifted_sum(encode(base_marks), stem_weight, stem_bias)).astype(jnp.bfloat16)
    padded = jnp.pad(pooled, ((reach_rows, reach_rows), (0, 0)))
    features = gelu_pool(shifted_sum(padded, conv_weight, conv_bias))
    normed = normalize(features, norm_gain)
    places = jnp.arange(TOKENS, dtype=jnp.int32)
    queries = rotate(jnp.dot(normed, query_weight, preferred_element_type=jnp.float32).reshape(TOKENS, HEADS, KD), places).astype(jnp.bfloat16)
    key_rows = rotate(jnp.dot(normed, key_weight, preferred_element_type=jnp.float32)[:, None, :], places)[:, 0, :].astype(jnp.bfloat16)
    value_rows = jnp.dot(normed, value_weight, preferred_element_type=jnp.float32).astype(jnp.bfloat16)
    score_scale = 1.0 / math.sqrt(KD)
    block_rows = math.gcd(TOKENS, 512)
    query_blocks = queries.reshape(TOKENS // block_rows, block_rows, HEADS, KD)
    key_float = key_rows.astype(jnp.float32)
    value_float = value_rows.astype(jnp.float32)

    def attend(query_block):
        raw_scores = jnp.einsum('qhd,kd->qhk', query_block.astype(jnp.float32), key_float) * score_scale
        capped = soft_cap * jnp.tanh(raw_scores / soft_cap)
        probability = jnp.exp(capped - soft_cap)
        totals = lax.optimization_barrier(jnp.sum(probability, axis=2))
        rounded = lax.optimization_barrier(probability.astype(jnp.bfloat16)).astype(jnp.float32)
        weighted = jnp.einsum('qhk,kv->qhv', rounded, value_float)
        return (weighted / totals[:, :, None]).astype(jnp.bfloat16)
    outputs = lax.map(attend, query_blocks)
    return outputs.reshape(TOKENS, HEADS * VD)
```

```python
import functools
import math

import jax
import jax.numpy as jnp
import numpy as np
from jax import lax
from jax.experimental import pallas as pl
from jax.experimental.pallas import tpu as pltpu
from jax.sharding import PartitionSpec as P

MESH = pl.DeviceIdType.MESH
SOFT_CAP = 20.0
ROPE_BASE = 10000.0
NX, NZ = 4, 16
TOK = 64
C1, C2, HEADS, KD, VD, TAPS = 384, 768, 8, 128, 192, 5
UROWS = 80
QROWS = TOK * HEADS
F32, BF16 = jnp.float32, jnp.bfloat16

U_C, U_R2, U_R1, U_L1, U_L2, U_O = 0, 2, 3, 4, 5, 6


def chunk(direction, step):
    if step == 0:
        return 0
    if step == 8:
        return 15
    return step if direction == 0 else 7 + step


def gelu(x):
    inner = math.sqrt(2.0 / math.pi) * (x + 0.044715 * (x * x * x))
    return (0.5 * x) * (1.0 + jnp.tanh(inner))


class Copies:
    def __init__(self, send, recv):
        self.send, self.recv, self.made = send, recv, []

    def start(self, src, dst, to):
        k = len(self.made)
        copy = pltpu.make_async_remote_copy(
            src_ref=src, dst_ref=dst, send_sem=self.send.at[k], recv_sem=self.recv.at[k],
            device_id={"seq": to}, device_id_type=MESH,
        )
        copy.start()
        self.made.append(copy)
        return copy


N_COPIES = 96


def kernel(
    bases_ref, stem_w_ref, stem_b_ref, conv_b_ref, gain_ref, rope_ref, step_ref,
    conv_w_hbm, query_w_hbm, key_w_hbm, value_w_hbm,
    out_ref,
    halo, onehot, stem_w, pooled_e, pooled_o, conv_in, conv_w, query_w, key_w, value_w,
    buf, q_buf, acc, tot, part, send, recv, load,
):
    me = lax.axis_index("seq")
    core, z, x = me % 2, (me // 2) % NZ, me // (2 * NZ)

    def at(xx, zz, cc):
        return ((xx % NX) * NZ + zz % NZ) * 2 + cc

    x_up, x_down = at(x + 1, z, core), at(x + NX - 1, z, core)
    z_up, z_down = at(x, z + 1, core), at(x, z + NZ - 1, core)
    twin = at(x, z, 1 - core)
    after, before = (me + 1) % (2 * NX * NZ), (me + 2 * NX * NZ - 1) % (2 * NX * NZ)
    other = jnp.where(core == 0, before, after)

    loads = [
        pltpu.make_async_copy(conv_w_hbm, conv_w, load.at[0]),
        pltpu.make_async_copy(key_w_hbm, key_w, load.at[1]),
        pltpu.make_async_copy(value_w_hbm, value_w.at[pl.ds(0, VD)], load.at[2]),
        pltpu.make_async_copy(value_w_hbm.at[pl.ds(KD, VD - KD)], value_w.at[pl.ds(VD, VD - KD)], load.at[3]),
        pltpu.make_async_copy(query_w_hbm, query_w, load.at[4]),
    ]
    for one in loads:
        one.start()

    barrier = pltpu.get_barrier_semaphore()
    for peer in (x_up, x_down, z_up, z_down, twin, other):
        pl.semaphore_signal(barrier, inc=1, device_id={"seq": peer}, device_id_type=MESH)
    pl.semaphore_wait(barrier, 6)

    copies = Copies(send, recv)
    from_before = copies.start(bases_ref, halo.at[0], after)
    from_after = copies.start(bases_ref, halo.at[1], before)

    stem_w[...] = jnp.zeros_like(stem_w)
    for t in range(TAPS):
        stem_w[t * 8 : t * 8 + 4, :] = stem_w_ref[t].astype(F32)
    dev = step_ref[pl.ds(me, 1), :]
    cos_d, sin_d = dev[:, :KD], dev[:, KD:]
    cos_r, sin_r = rope_ref[:, :KD], rope_ref[:, KD:]
    lane = lax.broadcasted_iota(jnp.int32, (TOK, KD), 1)
    cos = cos_d * cos_r - sin_d * sin_r
    sin = sin_d * cos_r + cos_d * sin_r
    sin = jnp.where(lane < KD // 2, -sin, sin)

    def rotate(u):
        return u * cos + pltpu.roll(u, KD // 2, 1) * sin

    from_before.wait_recv()
    from_after.wait_recv()

    lanes = lax.broadcasted_iota(jnp.int32, (8, 128), 1)
    left = jnp.where(me == 0, 0, pltpu.roll(halo[0], 66, 1))
    right = jnp.where(me == 2 * NX * NZ - 1, 0, pltpu.roll(halo[1], 66, 1))
    own = pltpu.roll(bases_ref[...], 2, 1)
    marks = jnp.where(lanes < 2, left, jnp.where(lanes < 66, own, jnp.where(lanes < 68, right, 0)))
    moved = [marks, pltpu.roll(marks, 127, 1), pltpu.roll(marks, 126, 1)]
    base = lax.broadcasted_iota(jnp.int32, (8, 128), 0) + 1
    for r in range(4):
        for t in range(TAPS):
            k = r + t - 2
            row = moved[1 + k // 4][k % 4 : k % 4 + 1, :]
            onehot[t * 8 : t * 8 + 8, r * 128 : (r + 1) * 128] = (
                jnp.broadcast_to(row, (8, 128)) == base
            ).astype(F32)
    stem = lax.dot_general(
        onehot[...].astype(BF16), stem_w[...].astype(BF16), (((0,), (0,)), ((), ())),
        preferred_element_type=F32,
    )
    stem = [gelu(stem[r * 128 : r * 128 + 72] + stem_b_ref[...]) for r in range(4)]
    spot = lax.broadcasted_iota(jnp.int32, (72, C1), 0)
    first = jnp.where(me == 0, 1, 0)
    last = jnp.where(me == 2 * NX * NZ - 1, 64, 65)
    inside = (spot >= first) & (spot <= last)
    pooled_e[...] = jnp.where(inside, jnp.maximum(stem[0], stem[1]), 0.0)
    pooled_o[...] = jnp.where(inside, jnp.maximum(stem[2], stem[3]), 0.0)

    shifted = [[ref[pl.ds(o, TOK), :].astype(BF16) for ref in (pooled_e, pooled_o)] for o in range(3)]
    for t in range(TAPS):
        conv_in[0:TOK, t * C1 : (t + 1) * C1] = shifted[t // 2][t % 2]
        conv_in[TOK : 2 * TOK, t * C1 : (t + 1) * C1] = shifted[(t + 1) // 2][(t + 1) % 2]
    loads[0].wait()
    conv = jnp.dot(
        conv_in[...], conv_w[...].reshape(TAPS * C1, C2), preferred_element_type=F32
    ) + conv_b_ref[...]
    conv = gelu(conv)
    features = jnp.maximum(conv[:TOK], conv[TOK:])
    mean_square = jnp.mean(features * features, axis=1, keepdims=True)
    normed = (features * lax.rsqrt(mean_square + 1e-06) * gain_ref[...]).astype(BF16)

    for one in loads[1:4]:
        one.wait()
    keys = rotate(jnp.dot(normed, key_w[...], preferred_element_type=F32)).astype(BF16)
    values = lax.dot_general(normed, value_w[...], (((1,), (1,)), ((), ())), preferred_element_type=F32)
    tails = values[:, KD:]
    values = values[:, :KD].astype(BF16)
    half = lax.broadcasted_iota(jnp.int32, (16, KD), 1) < KD // 2
    for u in range(2):
        buf[0, u, 0:32, :] = keys[u * 32 : u * 32 + 32]
        buf[0, u, 32:64, :] = values[u * 32 : u * 32 + 32]
        buf[0, u, 64:80, :] = jnp.where(
            half, tails[u * 32 : u * 32 + 16], tails[u * 32 + 16 : u * 32 + 32]
        ).astype(BF16)

    def units(c, u, n=1):
        return buf.at[c, pl.ds(u, n)]

    z_to = (z_up, z_down)
    arrive_a, arrive_b, arrive_x, arrive_o = {}, {}, {}, {}

    def send_a(direction, step):
        if step < 7 or (step == 7 and direction == 0):
            src, dst = chunk(direction, step), chunk(direction, step + 1)
            arrive_a[dst] = copies.start(units(src, U_C, 2), units(dst, U_C, 2), z_to[direction])

    def send_b(direction, step):
        if step < 7 or (step == 7 and direction == 1):
            src, dst = chunk(direction, step), chunk(direction, step + 1)
            arrive_b[dst] = copies.start(units(src, U_R1, 2), units(dst, U_R1, 2), z_to[direction])

    def send_x(c):
        arrive_x[c] = (
            copies.start(units(c, U_C + 1), units(c, U_L2), x_up),
            copies.start(units(c, U_C + 1), units(c, U_R2), x_down),
        )

    def send_o(c):
        if c in (0, 15):
            arrive_o[c] = (
                copies.start(units(c, U_L1), units(c, U_O), x_up),
                copies.start(units(c, U_R2), units(c, U_O + 1), x_down),
            )
        elif c < 8:
            arrive_o[c] = (copies.start(units(c, U_L1, 2), units(c, U_O, 2), x_up),)
        else:
            arrive_o[c] = (copies.start(units(c, U_R2, 2), units(c, U_O, 2), x_down),)

    arrive_b[0] = (
        copies.start(units(0, U_C), units(0, U_L1), x_up),
        copies.start(units(0, U_C), units(0, U_R1), x_down),
    )
    send_a(0, 0)
    send_a(1, 0)
    send_x(0)

    loads[4].wait()
    for h in range(HEADS):
        u = jnp.dot(normed, query_w[:, h * KD : (h + 1) * KD], preferred_element_type=F32)
        q_buf[0, h * TOK : (h + 1) * TOK, :] = rotate(u).astype(BF16)
        if h == 3:
            for copy in arrive_b[0]:
                copy.wait_recv()
            send_b(0, 0)
            send_b(1, 0)
    queries = copies.start(q_buf.at[0], q_buf.at[1], twin)
    for copy in arrive_x[0]:
        copy.wait_recv()
    send_o(0)

    acc[...] = jnp.zeros_like(acc)
    tot[...] = jnp.zeros_like(tot)

    scale = 1.0 / math.sqrt(KD) / SOFT_CAP
    peak = SOFT_CAP * math.log2(math.e)
    rows = 256

    def attend(c, owner):
        key_rows = buf[c, :, 0:32, :].reshape(256, KD)
        value_rows = buf[c, :, 32:64, :].reshape(256, KD)
        tail = buf[c, :, 64:80, :]
        turned = pltpu.roll(tail.astype(F32).reshape(128, KD), KD // 2, 1).astype(BF16).reshape(8, 16, KD)
        tail = jnp.concatenate([tail, turned], axis=1).reshape(256, KD)
        right_side = jnp.concatenate([value_rows, tail], axis=1)

        def body(i, carry):
            at_rows = pl.ds(pl.multiple_of(i * rows, rows), rows)
            scores = lax.dot_general(
                q_buf[owner, at_rows, :], key_rows, (((1,), (1,)), ((), ())), preferred_element_type=F32
            )
            probability = jnp.exp2(jnp.tanh(scores * scale) * peak - peak)
            tot[owner, at_rows, :] += probability[:, :128] + probability[:, 128:]
            acc[owner, at_rows, :] += jnp.dot(
                probability.astype(BF16), right_side, preferred_element_type=F32
            )
            return carry

        lax.fori_loop(0, QROWS // rows, body, 0)

    def complete(c):
        for copy in arrive_o[c]:
            copy.wait_recv()

    queries.wait_recv()
    for step in range(1, 9):
        pair = (chunk(0, step), chunk(1, step)) if step < 8 else (15,)
        ready = [] if step == 2 else [0] if step == 1 else [chunk(0, step - 2), chunk(1, step - 2)]
        for c in pair:
            direction = 0 if c < 8 or c == 15 else 1
            arrive_a[c].wait_recv()
            send_a(direction, step)
            send_x(c)
        if ready:
            complete(ready[0])
            attend(ready[0], 1)
        for c in pair:
            direction = 0 if c < 8 else 1
            arrive_b[c].wait_recv()
            send_b(direction, step)
        if ready:
            attend(ready[0], 0)
        if step > 1:
            for direction in (0, 1):
                c = chunk(direction, step - 1)
                for copy in arrive_x[c]:
                    copy.wait_recv()
                send_o(c)
        if len(ready) > 1:
            complete(ready[1])
            attend(ready[1], 1)
            attend(ready[1], 0)
    for copy in arrive_x[15]:
        copy.wait_recv()
    send_o(15)
    for c in (chunk(0, 7), chunk(1, 7)):
        complete(c)
        attend(c, 1)
        attend(c, 0)
    complete(15)
    attend(15, 1)

    def close(owner):
        wide = lax.broadcasted_iota(jnp.int32, (QROWS, 2 * KD), 1)
        total = jnp.sum(tot[owner], axis=1, keepdims=True)
        return jnp.where(wide < VD, acc[owner], total)

    acc[1] = close(1)
    home = copies.start(acc.at[1], part, twin)
    attend(15, 0)
    acc[0] = close(0)
    home.wait_recv()
    for h in range(HEADS):
        both = acc[0, h * TOK : (h + 1) * TOK, :] + part[h * TOK : (h + 1) * TOK, :]
        out_ref[:, h * VD : (h + 1) * VD] = (both[:, :VD] / both[:, VD : VD + 1]).astype(BF16)
    for copy in copies.made:
        copy.wait_send()
    assert len(copies.made) <= N_COPIES


def tables():
    frequency = np.exp(np.arange(KD // 2) * (-2.0 * math.log(ROPE_BASE) / KD))

    def both(places):
        angles = places[:, None] * frequency[None, :]
        return np.concatenate([np.cos(angles)] * 2 + [np.sin(angles)] * 2, axis=1).astype(np.float32)

    return both(np.arange(TOK)), both(np.arange(2 * NX * NZ) * TOK)


def on_device(
    dna_bases, stem_weight, stem_bias, conv_weight, conv_bias, norm_gain, query_weight, key_weight, value_weight
):
    marks = (dna_bases + 1).reshape(TOK, 4).T
    marks = jnp.pad(marks, ((0, 4), (0, 64)))
    rope, step = tables()
    vmem = pl.BlockSpec(memory_space=pltpu.VMEM)
    anywhere = pl.BlockSpec(memory_space=pl.ANY)
    return pl.pallas_call(
        kernel,
        out_shape=jax.ShapeDtypeStruct((TOK, HEADS * VD), BF16),
        in_specs=[vmem] * 7 + [anywhere] * 4,
        out_specs=vmem,
        scratch_shapes=[
            pltpu.VMEM((2, 8, 128), jnp.int32),
            pltpu.VMEM((40, 512), F32),
            pltpu.VMEM((40, C1), F32),
            pltpu.VMEM((72, C1), F32),
            pltpu.VMEM((72, C1), F32),
            pltpu.VMEM((2 * TOK, TAPS * C1), BF16),
            pltpu.VMEM((TAPS, C1, C2), BF16),
            pltpu.VMEM((C2, HEADS * KD), BF16),
            pltpu.VMEM((C2, KD), BF16),
            pltpu.VMEM((2 * KD, C2), BF16),
            pltpu.VMEM((16, 8, UROWS, 128), BF16),
            pltpu.VMEM((2, QROWS, KD), BF16),
            pltpu.VMEM((2, QROWS, 2 * KD), F32),
            pltpu.VMEM((2, QROWS, 128), F32),
            pltpu.VMEM((QROWS, 2 * KD), F32),
            pltpu.SemaphoreType.DMA((N_COPIES,)),
            pltpu.SemaphoreType.DMA((N_COPIES,)),
            pltpu.SemaphoreType.DMA((5,)),
        ],
        compiler_params=pltpu.CompilerParams(
            collective_id=0, has_side_effects=True, vmem_limit_bytes=48 << 20
        ),
    )(
        marks, stem_weight, stem_bias.reshape(1, C1), conv_bias.reshape(1, C2), norm_gain.reshape(1, C2),
        jnp.asarray(rope), jnp.asarray(step),
        conv_weight, query_weight, key_weight, value_weight.T,
    )


def solution(mesh):
    placed = (P(("batch", "seq")), P(), P(), P(), P(), P(), P(), P(), P())
    return jax.shard_map(
        on_device, mesh=mesh, in_specs=placed, out_specs=P(("batch", "seq"), None), check_vma=False
    )
```

```python
import functools
import math

import jax
import jax.numpy as jnp
import numpy as np
from jax import lax
from jax.experimental import pallas as pl
from jax.experimental.pallas import tpu as pltpu
from jax.sharding import PartitionSpec as P

MESH = pl.DeviceIdType.MESH
SOFT_CAP = 20.0
ROPE_BASE = 10000.0
NX, NZ = 4, 16
TOK = 64
C1, C2, HEADS, KD, VD, TAPS = 384, 768, 8, 128, 192, 5
UROWS = 80
QROWS = TOK * HEADS
F32, BF16 = jnp.float32, jnp.bfloat16

U_C, U_L2, U_L1, U_R1, U_R2, U_O = 0, 2, 3, 4, 5, 6

ORDER = (0, 1, -1, 2, -2, 5, -5, 4, -4, 6, -6, 3, -3, 7, -7, 8)
NEAR = (1, -1, 2, -2)


def gelu(x):
    inner = math.sqrt(2.0 / math.pi) * (x + 0.044715 * (x * x * x))
    return (0.5 * x) * (1.0 + jnp.tanh(inner))


class Copies:
    def __init__(self, send, recv):
        self.send, self.recv, self.made = send, recv, []

    def start(self, src, dst, to):
        k = len(self.made)
        copy = pltpu.make_async_remote_copy(
            src_ref=src, dst_ref=dst, send_sem=self.send.at[k], recv_sem=self.recv.at[k],
            device_id={"seq": to}, device_id_type=MESH,
        )
        copy.start()
        self.made.append(copy)
        return copy


N_COPIES = 96


def kernel(
    bases_hbm, stem_w_hbm, stem_b_hbm, conv_b_hbm, gain_hbm, rope_hbm, step_hbm,
    conv_w_hbm, query_w_hbm, key_w_hbm, value_w_hbm,
    out_ref,
    bases_ref, stem_w_ref, stem_b_ref, conv_b_ref, gain_ref, rope_ref, step_ref,
    halo, onehot, stem_w, pooled_e, pooled_o, conv_in, conv_w, query_w, key_w, value_w,
    buf, q_buf, acc, tot, part, send, recv, load,
):
    me = lax.axis_index("seq")
    core, z, x = me % 2, (me // 2) % NZ, me // (2 * NZ)

    def at(xx, zz, cc):
        return ((xx % NX) * NZ + zz % NZ) * 2 + cc

    x_up, x_down = at(x + 1, z, core), at(x + NX - 1, z, core)
    z_up, z_down = at(x, z + 1, core), at(x, z + NZ - 1, core)
    z_far_up, z_far_down = at(x, z + 5, core), at(x, z + NZ - 5, core)
    twin = at(x, z, 1 - core)
    after, before = (me + 1) % (2 * NX * NZ), (me + 2 * NX * NZ - 1) % (2 * NX * NZ)
    other = jnp.where(core == 0, before, after)

    first_loads = [
        pltpu.make_async_copy(bases_hbm.at[pl.ds(0, 128)], bases_ref.at[0], load.at[5]),
        pltpu.make_async_copy(bases_hbm.at[pl.ds(128, 128)], bases_ref.at[1], load.at[6]),
        pltpu.make_async_copy(stem_w_hbm, stem_w_ref, load.at[7]),
        pltpu.make_async_copy(stem_b_hbm, stem_b_ref, load.at[8]),
        pltpu.make_async_copy(rope_hbm, rope_ref, load.at[9]),
        pltpu.make_async_copy(step_hbm.at[pl.ds(me, 1)], step_ref, load.at[10]),
        pltpu.make_async_copy(conv_b_hbm, conv_b_ref, load.at[11]),
        pltpu.make_async_copy(gain_hbm, gain_ref, load.at[12]),
    ]
    for one in first_loads:
        one.start()
    loads = [
        pltpu.make_async_copy(conv_w_hbm, conv_w, load.at[0]),
        pltpu.make_async_copy(key_w_hbm, key_w, load.at[1]),
        pltpu.make_async_copy(value_w_hbm, value_w.at[pl.ds(0, VD)], load.at[2]),
        pltpu.make_async_copy(value_w_hbm.at[pl.ds(KD, VD - KD)], value_w.at[pl.ds(VD, VD - KD)], load.at[3]),
        pltpu.make_async_copy(query_w_hbm, query_w, load.at[4]),
    ]
    for one in loads:
        one.start()

    barrier = pltpu.get_barrier_semaphore()
    for peer in (x_up, x_down, z_up, z_down, z_far_up, z_far_down, twin, other):
        pl.semaphore_signal(barrier, inc=1, device_id={"seq": peer}, device_id_type=MESH)
    for one in first_loads:
        one.wait()
    pl.semaphore_wait(barrier, 8)

    copies = Copies(send, recv)
    from_before = copies.start(bases_ref, halo.at[0], after)
    from_after = copies.start(bases_ref, halo.at[1], before)

    stem_w[...] = jnp.zeros_like(stem_w)
    for t in range(TAPS):
        stem_w[t * 8 : t * 8 + 4, :] = stem_w_ref[t].astype(F32)
    dev = step_ref[...]
    cos_d, sin_d = dev[:, :KD], dev[:, KD:]
    cos_r, sin_r = rope_ref[:, :KD], rope_ref[:, KD:]
    lane = lax.broadcasted_iota(jnp.int32, (TOK, KD), 1)
    cos = cos_d * cos_r - sin_d * sin_r
    sin = sin_d * cos_r + cos_d * sin_r
    sin = jnp.where(lane < KD // 2, -sin, sin)

    def rotate(u):
        return u * cos + pltpu.roll(u, KD // 2, 1) * sin

    from_before.wait_recv()
    from_after.wait_recv()

    near = [
        jnp.where(me == 0, 0, halo[0, 1:2, :] + 1),
        bases_ref[0:1, :] + 1,
        bases_ref[1:2, :] + 1,
        jnp.where(me == 2 * NX * NZ - 1, 0, halo[1, 0:1, :] + 1),
    ]
    phase = (lax.broadcasted_iota(jnp.int32, (8, 128), 1) & 3) == lax.broadcasted_iota(jnp.int32, (8, 128), 0)
    spot = lax.broadcasted_iota(jnp.int32, (128, 128), 0)
    token = lax.broadcasted_iota(jnp.int32, (128, 128), 1)
    marks = jnp.zeros((8, 128), F32)
    for b in range(4):
        picked = jnp.where(phase, jnp.broadcast_to(near[b], (8, 128)), 0).astype(F32).astype(BF16)
        place = (((spot + (128 * b - 120)) >> 2) == token).astype(F32).astype(BF16)
        marks += jnp.dot(picked, place, preferred_element_type=F32)
    moved = [marks, pltpu.roll(marks, 127, 1), pltpu.roll(marks, 126, 1)]
    base = (lax.broadcasted_iota(jnp.int32, (8, 128), 0) + 1).astype(F32)
    for r in range(4):
        for t in range(TAPS):
            k = r + t - 2
            row = moved[1 + k // 4][k % 4 : k % 4 + 1, :]
            onehot[t * 8 : t * 8 + 8, r * 128 : (r + 1) * 128] = (
                jnp.broadcast_to(row, (8, 128)) == base
            ).astype(F32)
    stem = lax.dot_general(
        onehot[...].astype(BF16), stem_w[...].astype(BF16), (((0,), (0,)), ((), ())),
        preferred_element_type=F32,
    )
    stem = [gelu(stem[r * 128 : r * 128 + 72] + stem_b_ref[...].reshape(1, C1)) for r in range(4)]
    spot = lax.broadcasted_iota(jnp.int32, (72, C1), 0)
    first = jnp.where(me == 0, 1, 0)
    last = jnp.where(me == 2 * NX * NZ - 1, 64, 65)
    inside = (spot >= first) & (spot <= last)
    pooled_e[...] = jnp.where(inside, jnp.maximum(stem[0], stem[1]), 0.0)
    pooled_o[...] = jnp.where(inside, jnp.maximum(stem[2], stem[3]), 0.0)

    shifted = [[ref[pl.ds(o, TOK), :].astype(BF16) for ref in (pooled_e, pooled_o)] for o in range(3)]
    for t in range(TAPS):
        conv_in[0:TOK, t * C1 : (t + 1) * C1] = shifted[t // 2][t % 2]
        conv_in[TOK : 2 * TOK, t * C1 : (t + 1) * C1] = shifted[(t + 1) // 2][(t + 1) % 2]
    loads[0].wait()
    conv = jnp.dot(
        conv_in[...], conv_w[...].reshape(TAPS * C1, C2), preferred_element_type=F32
    ) + conv_b_ref[...].reshape(1, C2)
    conv = gelu(conv)
    features = jnp.maximum(conv[:TOK], conv[TOK:])
    mean_square = jnp.mean(features * features, axis=1, keepdims=True)
    normed = (features * lax.rsqrt(mean_square + 1e-06) * gain_ref[...].reshape(1, C2)).astype(BF16)

    for one in loads[1:4]:
        one.wait()
    keys = rotate(jnp.dot(normed, key_w[...], preferred_element_type=F32)).astype(BF16)
    values = lax.dot_general(normed, value_w[...], (((1,), (1,)), ((), ())), preferred_element_type=F32)
    tails = values[:, KD:]
    values = values[:, :KD].astype(BF16)
    half = lax.broadcasted_iota(jnp.int32, (16, KD), 1) < KD // 2
    for u in range(2):
        buf[0, u, 0:32, :] = keys[u * 32 : u * 32 + 32]
        buf[0, u, 32:64, :] = values[u * 32 : u * 32 + 32]
        buf[0, u, 64:80, :] = jnp.where(
            half, tails[u * 32 : u * 32 + 16], tails[u * 32 + 16 : u * 32 + 32]
        ).astype(BF16)

    def units(d, u, n=1):
        return buf.at[ORDER.index(d), pl.ds(u, n)]

    arrive_a, arrive_b, arrive_x, arrive_o = {}, {}, {}, {}

    def send_a(src, dst, to):
        arrive_a[dst] = copies.start(units(src, U_C, 2), units(dst, U_C, 2), to)

    def send_b(src, dst, to):
        u, n = (U_L1, 2) if dst in NEAR else (U_L1, 1) if 0 < dst < 8 else (U_R1, 1)
        arrive_b[dst] = copies.start(units(src, u, n), units(dst, u, n), to)

    def send_x(d):
        left, right = (U_C + 1, U_L2, 1), (U_C + 1, U_R2, 1)
        if 0 < d < 8 and d not in NEAR:
            right = (U_C, U_R1, 2)
        elif d not in NEAR:
            left = (U_C, U_L2, 2)
        arrive_x[d] = [
            copies.start(units(d, u, n), units(d, v, n), to)
            for (u, v, n), to in ((left, x_up), (right, x_down))
        ]

    def send_o(d):
        if d == 0:
            sends = ((U_L1, U_O, 1, x_up), (U_R2, U_O + 1, 1, x_down))
        elif 0 < d < 8:
            sends = ((U_L2, U_O, 2, x_up),)
        else:
            sends = ((U_R1, U_O, 2, x_down),)
        arrive_o[d] = [copies.start(units(d, u, n), units(d, v, n), to) for u, v, n, to in sends]

    def onward(d, send):
        if d in (1, 5, 6):
            send(d, d + 1, z_up)
        if d in (-1, -5, -6):
            send(d, d - 1, z_down)
        if d in (5, 4):
            send(d, d - 1, z_down)
        if d in (-5, -4):
            send(d, d + 1, z_up)
        if d == 7 and send is send_a:
            send(d, 8, z_up)
        if d == -7 and send is send_b:
            send(d, 8, z_down)

    send_a(0, 5, z_far_up)
    send_a(0, -5, z_far_down)
    arrive_x[0] = [
        copies.start(units(0, u, n), units(0, v, n), to)
        for u, v, n, to in ((U_C, U_L1, 1, x_up), (U_C, U_R1, 2, x_down), (U_C + 1, U_L2, 1, x_up))
    ]
    send_a(0, 1, z_up)
    send_a(0, -1, z_down)

    def take_a(*chunks):
        for d in chunks:
            arrive_a[d].wait_recv()
            onward(d, send_a)
            send_x(d)

    def take_b(*chunks):
        for d in chunks:
            arrive_b[d].wait_recv()
            onward(d, send_b)

    def take_x(*chunks):
        for d in chunks:
            for copy in arrive_x[d]:
                copy.wait_recv()
            send_o(d)

    loads[4].wait()
    for h in range(HEADS):
        u = jnp.dot(normed, query_w[:, h * KD : (h + 1) * KD], preferred_element_type=F32)
        q_buf[h * TOK : (h + 1) * TOK, :] = rotate(u).astype(BF16)
    queries = copies.start(q_buf.at[pl.ds(0, QROWS)], q_buf.at[pl.ds(QROWS, QROWS)], twin)

    take_x(0)
    send_b(0, 5, z_far_up)
    send_b(0, -5, z_far_down)
    send_b(0, 1, z_up)
    send_b(0, -1, z_down)
    take_a(1, -1)
    acc[...] = jnp.zeros_like(acc)
    tot[...] = jnp.zeros_like(tot)
    queries.wait_recv()

    scale = 1.0 / math.sqrt(KD) / SOFT_CAP
    peak = SOFT_CAP * math.log2(math.e)
    rows, width = 256, 512

    def attend(tile, blocks):
        for d in ORDER[2 * tile : 2 * tile + 2]:
            for copy in arrive_o.pop(d, ()):
                copy.wait_recv()
        key_rows = buf[2 * tile : 2 * tile + 2, :, 0:32, :].reshape(width, KD)
        value_rows = buf[2 * tile : 2 * tile + 2, :, 32:64, :].reshape(width, KD)
        tail = buf[2 * tile : 2 * tile + 2, :, 64:80, :].reshape(width // 32, 16, KD)
        turned = pltpu.roll(tail.astype(F32).reshape(width // 2, KD), KD // 2, 1)
        turned = turned.astype(BF16).reshape(width // 32, 16, KD)
        tail = jnp.concatenate([tail, turned], axis=1).reshape(width, KD)
        right_side = jnp.concatenate([value_rows, tail], axis=1)
        for i in blocks:
            at_rows = pl.ds(i * rows, rows)
            scores = lax.dot_general(
                q_buf[at_rows, :], key_rows, (((1,), (1,)), ((), ())), preferred_element_type=F32
            )
            probability = jnp.exp2(jnp.tanh(scores * scale) * peak - peak)
            tot[at_rows, :] += sum(probability[:, j : j + 128] for j in range(0, width, 128))
            acc[at_rows, :] += jnp.dot(probability.astype(BF16), right_side, preferred_element_type=F32)

    every = range(2 * QROWS // rows)
    take_a(5, -5, 2, -2)
    take_b(1, -1)
    take_x(1, -1)
    take_a(6, -6, 4, -4)
    take_b(5, -5, 2, -2)
    take_x(5, -5, 2, -2)
    attend(0, every)
    take_a(7, -7, 3, -3)
    take_b(6, -6, 4, -4)
    take_x(6, -6, 4, -4)
    attend(1, every)
    attend(2, every)
    take_a(8)
    take_b(7, -7, 3, -3)
    take_x(7, -7, 3, -3)
    attend(3, every)
    attend(4, every)
    take_b(8)
    take_x(8)
    attend(5, every)
    attend(6, every)

    wide = lax.broadcasted_iota(jnp.int32, (rows, 2 * KD), 1)
    home = []
    for i in (2, 3):
        attend(7, (i,))
        at_rows = pl.ds(i * rows, rows)
        total = jnp.sum(tot[at_rows, :], axis=1, keepdims=True)
        acc[at_rows, :] = jnp.where(wide < VD, acc[at_rows, :], total)
        home.append(copies.start(acc.at[at_rows], part.at[pl.ds((i - 2) * rows, rows)], twin))
    attend(7, (0, 1))
    for h in range(HEADS):
        if h % 4 == 0:
            home[h // 4].wait_recv()
        at_rows = pl.ds(h * TOK, TOK)
        both = acc[at_rows, :VD] + part[at_rows, :VD]
        total = jnp.sum(tot[at_rows, :], axis=1, keepdims=True) + part[at_rows, VD : VD + 1]
        out_ref[:, h * VD : (h + 1) * VD] = (both * (1.0 / total)).astype(BF16)
    for copy in copies.made:
        copy.wait_send()
    assert len(copies.made) <= N_COPIES


def tables():
    frequency = np.exp(np.arange(KD // 2) * (-2.0 * math.log(ROPE_BASE) / KD))

    def both(places):
        angles = places[:, None] * frequency[None, :]
        return np.concatenate([np.cos(angles)] * 2 + [np.sin(angles)] * 2, axis=1).astype(np.float32)

    return both(np.arange(TOK)), both(np.arange(2 * NX * NZ) * TOK)


def on_device(
    dna_bases, stem_weight, stem_bias, conv_weight, conv_bias, norm_gain, query_weight, key_weight, value_weight
):
    rope, step = tables()
    vmem = pl.BlockSpec(memory_space=pltpu.VMEM)
    anywhere = pl.BlockSpec(memory_space=pl.ANY)
    return pl.pallas_call(
        kernel,
        out_shape=jax.ShapeDtypeStruct((TOK, HEADS * VD), BF16),
        in_specs=[anywhere] * 11,
        out_specs=vmem,
        scratch_shapes=[
            pltpu.VMEM((2, 128), jnp.int32),
            pltpu.VMEM((TAPS, 4, C1), BF16),
            pltpu.VMEM((C1,), F32),
            pltpu.VMEM((C2,), F32),
            pltpu.VMEM((C2,), F32),
            pltpu.VMEM((TOK, 2 * KD), F32),
            pltpu.VMEM((1, 2 * KD), F32),
            pltpu.VMEM((2, 2, 128), jnp.int32),
            pltpu.VMEM((40, 512), F32),
            pltpu.VMEM((40, C1), F32),
            pltpu.VMEM((72, C1), F32),
            pltpu.VMEM((72, C1), F32),
            pltpu.VMEM((2 * TOK, TAPS * C1), BF16),
            pltpu.VMEM((TAPS, C1, C2), BF16),
            pltpu.VMEM((C2, HEADS * KD), BF16),
            pltpu.VMEM((C2, KD), BF16),
            pltpu.VMEM((2 * KD, C2), BF16),
            pltpu.VMEM((16, 8, UROWS, 128), BF16),
            pltpu.VMEM((2 * QROWS, KD), BF16),
            pltpu.VMEM((2 * QROWS, 2 * KD), F32),
            pltpu.VMEM((2 * QROWS, 128), F32),
            pltpu.VMEM((QROWS, 2 * KD), F32),
            pltpu.SemaphoreType.DMA((N_COPIES,)),
            pltpu.SemaphoreType.DMA((N_COPIES,)),
            pltpu.SemaphoreType.DMA((13,)),
        ],
        compiler_params=pltpu.CompilerParams(
            collective_id=0, has_side_effects=True, vmem_limit_bytes=62 << 20
        ),
    )(
        dna_bases, stem_weight, stem_bias, conv_bias, norm_gain,
        jnp.asarray(rope), jnp.asarray(step),
        conv_weight, query_weight, key_weight, value_weight.T,
    )


def solution(mesh):
    placed = (P(("batch", "seq")), P(), P(), P(), P(), P(), P(), P(), P())
    return jax.shard_map(
        on_device, mesh=mesh, in_specs=placed, out_specs=P(("batch", "seq"), None), check_vma=False
    )
```

```python
import functools
import math

import jax
import jax.numpy as jnp
import numpy as np
from jax import lax
from jax.experimental import pallas as pl
from jax.experimental.pallas import tpu as pltpu
from jax.sharding import PartitionSpec as P

MESH = pl.DeviceIdType.MESH
SOFT_CAP = 20.0
ROPE_BASE = 10000.0
NX, NZ = 4, 16
TOK = 64
C1, C2, HEADS, KD, VD, TAPS = 384, 768, 8, 128, 192, 5
UROWS = 80
QROWS = TOK * HEADS
F32, BF16 = jnp.float32, jnp.bfloat16

U_C, U_L2, U_L1, U_R1, U_R2, U_O = 0, 2, 3, 4, 5, 6

ORDER = (0, 1, -1, 5, -5, 2, -2, 6, -6, 4, -4, 7, -7, 3, -3, 8)
NEAR = (1, -1, 2, -2)
SEED = 5
STAGES = ((1, -1), (5, -5, 2, -2), (6, -6, 4, -4), (7, -7, 3, -3), (8,))
UP, BACK = {1: 2, 5: 6, 6: 7}, {5: 4, 4: 3}


def gelu(x):
    inner = math.sqrt(2.0 / math.pi) * (x + 0.044715 * (x * x * x))
    return (0.5 * x) * (1.0 + jnp.tanh(inner))


class Copies:
    def __init__(self, send, recv):
        self.send, self.recv, self.made = send, recv, []

    def start(self, src, dst, to):
        k = len(self.made)
        copy = pltpu.make_async_remote_copy(
            src_ref=src, dst_ref=dst, send_sem=self.send.at[k], recv_sem=self.recv.at[k],
            device_id={"seq": to}, device_id_type=MESH,
        )
        copy.start()
        self.made.append(copy)
        return copy


N_COPIES = 96


def kernel(
    bases_hbm, stem_w_hbm, stem_b_hbm, conv_b_hbm, gain_hbm, rope_hbm, step_hbm,
    conv_w_hbm, query_w_hbm, key_w_hbm, value_w_hbm,
    out_ref,
    bases_ref, stem_w_ref, stem_b_ref, conv_b_ref, gain_ref, rope_ref, step_ref,
    halo, onehot, stem_w, pooled_e, pooled_o, conv_in, conv_w, query_w, key_w, value_w,
    buf, q_buf, acc, tot, part, send, recv, load,
):
    me = lax.axis_index("seq")
    core, z, x = me % 2, (me // 2) % NZ, me // (2 * NZ)

    def at(xx, zz, cc):
        return ((xx % NX) * NZ + zz % NZ) * 2 + cc

    x_up, x_down = at(x + 1, z, core), at(x + NX - 1, z, core)
    z_up, z_down = at(x, z + 1, core), at(x, z + NZ - 1, core)
    z_far_up, z_far_down = at(x, z + SEED, core), at(x, z + NZ - SEED, core)
    twin = at(x, z, 1 - core)
    after, before = (me + 1) % (2 * NX * NZ), (me + 2 * NX * NZ - 1) % (2 * NX * NZ)
    other = jnp.where(core == 0, before, after)

    first_loads = [
        pltpu.make_async_copy(bases_hbm.at[pl.ds(0, 128)], bases_ref.at[0], load.at[5]),
        pltpu.make_async_copy(bases_hbm.at[pl.ds(128, 128)], bases_ref.at[1], load.at[6]),
        pltpu.make_async_copy(stem_w_hbm, stem_w_ref, load.at[7]),
        pltpu.make_async_copy(stem_b_hbm, stem_b_ref, load.at[8]),
        pltpu.make_async_copy(rope_hbm, rope_ref, load.at[9]),
        pltpu.make_async_copy(step_hbm.at[pl.ds(me, 1)], step_ref, load.at[10]),
        pltpu.make_async_copy(conv_b_hbm, conv_b_ref, load.at[11]),
        pltpu.make_async_copy(gain_hbm, gain_ref, load.at[12]),
    ]
    for one in first_loads:
        one.start()
    loads = [
        pltpu.make_async_copy(conv_w_hbm, conv_w, load.at[0]),
        pltpu.make_async_copy(key_w_hbm, key_w, load.at[1]),
        pltpu.make_async_copy(value_w_hbm, value_w.at[pl.ds(0, VD)], load.at[2]),
        pltpu.make_async_copy(value_w_hbm.at[pl.ds(KD, VD - KD)], value_w.at[pl.ds(VD, VD - KD)], load.at[3]),
        pltpu.make_async_copy(query_w_hbm, query_w, load.at[4]),
    ]
    for one in loads:
        one.start()

    barrier = pltpu.get_barrier_semaphore()
    for peer in (x_up, x_down, z_up, z_down, z_far_up, z_far_down, twin, other):
        pl.semaphore_signal(barrier, inc=1, device_id={"seq": peer}, device_id_type=MESH)
    for one in first_loads:
        one.wait()
    pl.semaphore_wait(barrier, 8)

    copies = Copies(send, recv)
    from_before = copies.start(bases_ref, halo.at[0], after)
    from_after = copies.start(bases_ref, halo.at[1], before)

    stem_w[...] = jnp.zeros_like(stem_w)
    for t in range(TAPS):
        stem_w[t * 8 : t * 8 + 4, :] = stem_w_ref[t].astype(F32)
    dev = step_ref[...]
    cos_d, sin_d = dev[:, :KD], dev[:, KD:]
    cos_r, sin_r = rope_ref[:, :KD], rope_ref[:, KD:]
    lane = lax.broadcasted_iota(jnp.int32, (TOK, KD), 1)
    cos = cos_d * cos_r - sin_d * sin_r
    sin = sin_d * cos_r + cos_d * sin_r
    sin = jnp.where(lane < KD // 2, -sin, sin)

    def rotate(u):
        return u * cos + pltpu.roll(u, KD // 2, 1) * sin

    from_before.wait_recv()
    from_after.wait_recv()

    near = [
        jnp.where(me == 0, 0, halo[0, 1:2, :] + 1),
        bases_ref[0:1, :] + 1,
        bases_ref[1:2, :] + 1,
        jnp.where(me == 2 * NX * NZ - 1, 0, halo[1, 0:1, :] + 1),
    ]
    phase = (lax.broadcasted_iota(jnp.int32, (8, 128), 1) & 3) == lax.broadcasted_iota(jnp.int32, (8, 128), 0)
    spot = lax.broadcasted_iota(jnp.int32, (128, 128), 0)
    token = lax.broadcasted_iota(jnp.int32, (128, 128), 1)
    marks = jnp.zeros((8, 128), F32)
    for b in range(4):
        picked = jnp.where(phase, jnp.broadcast_to(near[b], (8, 128)), 0).astype(F32).astype(BF16)
        place = (((spot + (128 * b - 120)) >> 2) == token).astype(F32).astype(BF16)
        marks += jnp.dot(picked, place, preferred_element_type=F32)
    moved = [marks, pltpu.roll(marks, 127, 1), pltpu.roll(marks, 126, 1)]
    base = (lax.broadcasted_iota(jnp.int32, (8, 128), 0) + 1).astype(F32)
    for r in range(4):
        for t in range(TAPS):
            k = r + t - 2
            row = moved[1 + k // 4][k % 4 : k % 4 + 1, :]
            onehot[t * 8 : t * 8 + 8, r * 128 : (r + 1) * 128] = (
                jnp.broadcast_to(row, (8, 128)) == base
            ).astype(F32)
    stem = lax.dot_general(
        onehot[...].astype(BF16), stem_w[...].astype(BF16), (((0,), (0,)), ((), ())),
        preferred_element_type=F32,
    )
    stem = [gelu(stem[r * 128 : r * 128 + 72] + stem_b_ref[...].reshape(1, C1)) for r in range(4)]
    spot = lax.broadcasted_iota(jnp.int32, (72, C1), 0)
    first = jnp.where(me == 0, 1, 0)
    last = jnp.where(me == 2 * NX * NZ - 1, 64, 65)
    inside = (spot >= first) & (spot <= last)
    pooled_e[...] = jnp.where(inside, jnp.maximum(stem[0], stem[1]), 0.0)
    pooled_o[...] = jnp.where(inside, jnp.maximum(stem[2], stem[3]), 0.0)

    shifted = [[ref[pl.ds(o, TOK), :].astype(BF16) for ref in (pooled_e, pooled_o)] for o in range(3)]
    for t in range(TAPS):
        conv_in[0:TOK, t * C1 : (t + 1) * C1] = shifted[t // 2][t % 2]
        conv_in[TOK : 2 * TOK, t * C1 : (t + 1) * C1] = shifted[(t + 1) // 2][(t + 1) % 2]
    loads[0].wait()
    conv = jnp.dot(
        conv_in[...], conv_w[...].reshape(TAPS * C1, C2), preferred_element_type=F32
    ) + conv_b_ref[...].reshape(1, C2)
    conv = gelu(conv)
    features = jnp.maximum(conv[:TOK], conv[TOK:])
    mean_square = jnp.mean(features * features, axis=1, keepdims=True)
    normed = (features * lax.rsqrt(mean_square + 1e-06) * gain_ref[...].reshape(1, C2)).astype(BF16)

    for one in loads[1:4]:
        one.wait()
    keys = rotate(jnp.dot(normed, key_w[...], preferred_element_type=F32)).astype(BF16)
    values = lax.dot_general(normed, value_w[...], (((1,), (1,)), ((), ())), preferred_element_type=F32)
    tails = values[:, KD:]
    values = values[:, :KD].astype(BF16)
    half = lax.broadcasted_iota(jnp.int32, (16, KD), 1) < KD // 2
    for u in range(2):
        buf[0, u, 0:32, :] = keys[u * 32 : u * 32 + 32]
        buf[0, u, 32:64, :] = values[u * 32 : u * 32 + 32]
        buf[0, u, 64:80, :] = jnp.where(
            half, tails[u * 32 : u * 32 + 16], tails[u * 32 + 16 : u * 32 + 32]
        ).astype(BF16)

    def units(d, u, n=1):
        return buf.at[ORDER.index(d), pl.ds(u, n)]

    arrive_a, arrive_b, arrive_x, arrive_o = {}, {}, {}, {}

    def send_a(src, dst, to):
        arrive_a[dst] = copies.start(units(src, U_C, 2), units(dst, U_C, 2), to)

    def send_b(src, dst, to):
        u, n = (U_L1, 2) if dst in NEAR else (U_L1, 1) if 0 < dst < 8 else (U_R1, 1)
        arrive_b[dst] = copies.start(units(src, u, n), units(dst, u, n), to)

    def send_x(d):
        left, right = (U_C + 1, U_L2, 1), (U_C + 1, U_R2, 1)
        if 0 < d < 8 and d not in NEAR:
            right = (U_C, U_R1, 2)
        elif d not in NEAR:
            left = (U_C, U_L2, 2)
        arrive_x[d] = [
            copies.start(units(d, u, n), units(d, v, n), to)
            for (u, v, n), to in ((left, x_up), (right, x_down))
        ]

    def send_o(d):
        if d == 0:
            sends = ((U_L1, U_O, 1, x_up), (U_R2, U_O + 1, 1, x_down))
        elif 0 < d < 8:
            sends = ((U_L2, U_O, 2, x_up),)
        else:
            sends = ((U_R1, U_O, 2, x_down),)
        arrive_o[d] = [copies.start(units(d, u, n), units(d, v, n), to) for u, v, n, to in sends]

    def onward(d, send):
        away, back = (z_up, z_down) if d > 0 else (z_down, z_up)
        sign = 1 if d > 0 else -1
        if abs(d) in UP:
            send(d, sign * UP[abs(d)], away)
        if abs(d) in BACK:
            send(d, sign * BACK[abs(d)], back)
        if d == (7 if send is send_a else -7):
            send(d, 8, away)

    send_a(0, SEED, z_far_up)
    send_a(0, -SEED, z_far_down)
    arrive_x[0] = [
        copies.start(units(0, u, n), units(0, v, n), to)
        for u, v, n, to in ((U_C, U_L1, 1, x_up), (U_C, U_R1, 2, x_down), (U_C + 1, U_L2, 1, x_up))
    ]
    send_a(0, 1, z_up)
    send_a(0, -1, z_down)

    def take_a(*chunks):
        for d in chunks:
            arrive_a[d].wait_recv()
            onward(d, send_a)
            send_x(d)

    def take_b(*chunks):
        for d in chunks:
            arrive_b[d].wait_recv()
            onward(d, send_b)

    def take_x(*chunks):
        for d in chunks:
            for copy in arrive_x[d]:
                copy.wait_recv()
            send_o(d)

    loads[4].wait()
    for h in range(HEADS):
        u = jnp.dot(normed, query_w[:, h * KD : (h + 1) * KD], preferred_element_type=F32)
        q_buf[h * TOK : (h + 1) * TOK, :] = rotate(u).astype(BF16)
    queries = copies.start(q_buf.at[pl.ds(0, QROWS)], q_buf.at[pl.ds(QROWS, QROWS)], twin)

    take_x(0)
    send_b(0, SEED, z_far_up)
    send_b(0, -SEED, z_far_down)
    send_b(0, 1, z_up)
    send_b(0, -1, z_down)
    take_a(*STAGES[0])
    acc[...] = jnp.zeros_like(acc)
    tot[...] = jnp.zeros_like(tot)
    queries.wait_recv()

    scale = 1.0 / math.sqrt(KD) / SOFT_CAP
    peak = SOFT_CAP * math.log2(math.e)
    rows, width = 256, 512

    def attend(tile, blocks):
        for d in ORDER[2 * tile : 2 * tile + 2]:
            for copy in arrive_o.pop(d, ()):
                copy.wait_recv()
        key_rows = buf[2 * tile : 2 * tile + 2, :, 0:32, :].reshape(width, KD)
        value_rows = buf[2 * tile : 2 * tile + 2, :, 32:64, :].reshape(width, KD)
        tail = buf[2 * tile : 2 * tile + 2, :, 64:80, :].reshape(width // 32, 16, KD)
        turned = pltpu.roll(tail.astype(F32).reshape(width // 2, KD), KD // 2, 1)
        turned = turned.astype(BF16).reshape(width // 32, 16, KD)
        tail = jnp.concatenate([tail, turned], axis=1).reshape(width, KD)
        right_side = jnp.concatenate([value_rows, tail], axis=1)
        for i in blocks:
            at_rows = pl.ds(i * rows, rows)
            scores = lax.dot_general(
                q_buf[at_rows, :], key_rows, (((1,), (1,)), ((), ())), preferred_element_type=F32
            )
            probability = jnp.exp2(jnp.tanh(scores * scale) * peak - peak)
            tot[at_rows, :] += sum(probability[:, j : j + 128] for j in range(0, width, 128))
            acc[at_rows, :] += jnp.dot(probability.astype(BF16), right_side, preferred_element_type=F32)

    every = range(2 * QROWS // rows)
    tile = 0
    for k in range(1, len(STAGES) + 1):
        if k < len(STAGES):
            take_a(*STAGES[k])
        take_b(*STAGES[k - 1])
        take_x(*STAGES[k - 1])
        known = 1 + sum(len(stage) for stage in STAGES[: k - 1])
        while tile < min(known // 2, 7):
            attend(tile, every)
            tile += 1
    while tile < 7:
        attend(tile, every)
        tile += 1

    wide = lax.broadcasted_iota(jnp.int32, (rows, 2 * KD), 1)
    home = []
    for i in (2, 3):
        attend(7, (i,))
        at_rows = pl.ds(i * rows, rows)
        total = jnp.sum(tot[at_rows, :], axis=1, keepdims=True)
        acc[at_rows, :] = jnp.where(wide < VD, acc[at_rows, :], total)
        home.append(copies.start(acc.at[at_rows], part.at[pl.ds((i - 2) * rows, rows)], twin))
    attend(7, (0, 1))
    for h in range(HEADS):
        if h % 4 == 0:
            home[h // 4].wait_recv()
        at_rows = pl.ds(h * TOK, TOK)
        both = acc[at_rows, :VD] + part[at_rows, :VD]
        total = jnp.sum(tot[at_rows, :], axis=1, keepdims=True) + part[at_rows, VD : VD + 1]
        out_ref[:, h * VD : (h + 1) * VD] = (both * (1.0 / total)).astype(BF16)
    for copy in copies.made:
        copy.wait_send()
    assert len(copies.made) <= N_COPIES


def tables():
    frequency = np.exp(np.arange(KD // 2) * (-2.0 * math.log(ROPE_BASE) / KD))

    def both(places):
        angles = places[:, None] * frequency[None, :]
        return np.concatenate([np.cos(angles)] * 2 + [np.sin(angles)] * 2, axis=1).astype(np.float32)

    return both(np.arange(TOK)), both(np.arange(2 * NX * NZ) * TOK)


def on_device(
    dna_bases, stem_weight, stem_bias, conv_weight, conv_bias, norm_gain, query_weight, key_weight, value_weight
):
    rope, step = tables()
    vmem = pl.BlockSpec(memory_space=pltpu.VMEM)
    anywhere = pl.BlockSpec(memory_space=pltpu.HBM)
    return pl.pallas_call(
        kernel,
        out_shape=jax.ShapeDtypeStruct((TOK, HEADS * VD), BF16),
        in_specs=[anywhere] * 11,
        out_specs=vmem,
        scratch_shapes=[
            pltpu.VMEM((2, 128), jnp.int32),
            pltpu.VMEM((TAPS, 4, C1), BF16),
            pltpu.VMEM((C1,), F32),
            pltpu.VMEM((C2,), F32),
            pltpu.VMEM((C2,), F32),
            pltpu.VMEM((TOK, 2 * KD), F32),
            pltpu.VMEM((1, 2 * KD), F32),
            pltpu.VMEM((2, 2, 128), jnp.int32),
            pltpu.VMEM((40, 512), F32),
            pltpu.VMEM((40, C1), F32),
            pltpu.VMEM((72, C1), F32),
            pltpu.VMEM((72, C1), F32),
            pltpu.VMEM((2 * TOK, TAPS * C1), BF16),
            pltpu.VMEM((TAPS, C1, C2), BF16),
            pltpu.VMEM((C2, HEADS * KD), BF16),
            pltpu.VMEM((C2, KD), BF16),
            pltpu.VMEM((2 * KD, C2), BF16),
            pltpu.VMEM((16, 8, UROWS, 128), BF16),
            pltpu.VMEM((2 * QROWS, KD), BF16),
            pltpu.VMEM((2 * QROWS, 2 * KD), F32),
            pltpu.VMEM((2 * QROWS, 128), F32),
            pltpu.VMEM((QROWS, 2 * KD), F32),
            pltpu.SemaphoreType.DMA((N_COPIES,)),
            pltpu.SemaphoreType.DMA((N_COPIES,)),
            pltpu.SemaphoreType.DMA((13,)),
        ],
        compiler_params=pltpu.CompilerParams(
            collective_id=0, has_side_effects=True, vmem_limit_bytes=44 << 20
        ),
    )(*(
        pltpu.with_memory_space_constraint(one, pltpu.HBM)
        for one in (
            dna_bases, stem_weight, stem_bias, conv_bias, norm_gain, jnp.asarray(rope), jnp.asarray(step),
            conv_weight, query_weight, key_weight, value_weight.T,
        )
    ))


def solution(mesh):
    placed = (P(("batch", "seq")), P(), P(), P(), P(), P(), P(), P(), P())
    return jax.shard_map(
        on_device, mesh=mesh, in_specs=placed, out_specs=P(("batch", "seq"), None), check_vma=False
    )
```

```python
import functools
import math

import jax
import jax.numpy as jnp
import numpy as np
from jax import lax
from jax.experimental import pallas as pl
from jax.experimental.pallas import tpu as pltpu
from jax.sharding import PartitionSpec as P

MESH = pl.DeviceIdType.MESH
SOFT_CAP = 20.0
ROPE_BASE = 10000.0
NX, NZ = 4, 16
TOK = 64
C1, C2, HEADS, KD, VD, TAPS = 384, 768, 8, 128, 192, 5
UROWS = 80
QROWS = TOK * HEADS
F32, BF16 = jnp.float32, jnp.bfloat16

U_C, U_L, U_R, U_O = 0, 2, 4, 6

ORDER = (0, 1, -1, 5, -5, 2, -2, 6, -6, 4, -4, 7, -7, 3, -3, 8)
OVER_Z = {1: 2, -1: 2, 2: 2, -2: 2, 5: 2, -5: 2, 6: 4, -6: 4, 4: 4, -4: 4, 7: 4, -7: 4, 3: 4, -3: 4, 8: 2}
SEED = 5
STAGES = ((1, -1), (5, -5, 2, -2), (6, -6, 4, -4), (7, -7, 3, -3, 8))
UP, BACK = {1: 2, 5: 6, 6: 7}, {5: 4, 4: 3}


def over_z(d):
    ahead = 0 < d < 8
    return {
        2: (U_L, 0), 3: (U_L + 1, 1) if ahead else (U_R, 1), 4: (U_L + 1, 2), 5: (U_L, 3) if ahead else (U_L + 1, 3)
    }[OVER_Z.get(d, 2)]


def covers(src, dst):
    (u, n), (v, m) = over_z(src), over_z(dst)
    return src != 0 and u <= v and v + m <= u + n


def gelu(x):
    inner = math.sqrt(2.0 / math.pi) * (x + 0.044715 * (x * x * x))
    return (0.5 * x) * (1.0 + jnp.tanh(inner))


class Copies:
    def __init__(self, send, recv):
        self.send, self.recv, self.made = send, recv, []

    def start(self, src, dst, to):
        k = len(self.made)
        copy = pltpu.make_async_remote_copy(
            src_ref=src, dst_ref=dst, send_sem=self.send.at[k], recv_sem=self.recv.at[k],
            device_id={"seq": to}, device_id_type=MESH,
        )
        copy.start()
        self.made.append(copy)
        return copy


N_COPIES = 96


def kernel(
    bases_hbm, stem_w_hbm, stem_b_hbm, conv_b_hbm, gain_hbm, rope_hbm, step_hbm,
    conv_w_hbm, query_w_hbm, key_w_hbm, value_w_hbm,
    out_ref,
    bases_ref, stem_w_ref, stem_b_ref, conv_b_ref, gain_ref, rope_ref, step_ref,
    halo, onehot, stem_w, pooled_e, pooled_o, conv_in, conv_w, query_w, key_w, value_w,
    buf, q_buf, acc, tot, part, send, recv, load,
):
    me = lax.axis_index("seq")
    core, z, x = me % 2, (me // 2) % NZ, me // (2 * NZ)

    def at(xx, zz, cc):
        return ((xx % NX) * NZ + zz % NZ) * 2 + cc

    x_up, x_down = at(x + 1, z, core), at(x + NX - 1, z, core)
    z_up, z_down = at(x, z + 1, core), at(x, z + NZ - 1, core)
    z_far_up, z_far_down = at(x, z + SEED, core), at(x, z + NZ - SEED, core)
    z_three_up, z_three_down = at(x, z + 8 - SEED, core), at(x, z + NZ - 8 + SEED, core)
    twin = at(x, z, 1 - core)
    after, before = (me + 1) % (2 * NX * NZ), (me + 2 * NX * NZ - 1) % (2 * NX * NZ)
    other = jnp.where(core == 0, before, after)

    first_loads = [
        pltpu.make_async_copy(bases_hbm.at[pl.ds(0, 128)], bases_ref.at[0], load.at[5]),
        pltpu.make_async_copy(bases_hbm.at[pl.ds(128, 128)], bases_ref.at[1], load.at[6]),
        pltpu.make_async_copy(stem_w_hbm, stem_w_ref, load.at[7]),
        pltpu.make_async_copy(stem_b_hbm, stem_b_ref, load.at[8]),
        pltpu.make_async_copy(rope_hbm, rope_ref, load.at[9]),
        pltpu.make_async_copy(step_hbm.at[pl.ds(me, 1)], step_ref, load.at[10]),
        pltpu.make_async_copy(conv_b_hbm, conv_b_ref, load.at[11]),
        pltpu.make_async_copy(gain_hbm, gain_ref, load.at[12]),
    ]
    for one in first_loads:
        one.start()
    loads = [
        pltpu.make_async_copy(conv_w_hbm, conv_w, load.at[0]),
        pltpu.make_async_copy(key_w_hbm, key_w, load.at[1]),
        pltpu.make_async_copy(value_w_hbm, value_w.at[pl.ds(0, VD)], load.at[2]),
        pltpu.make_async_copy(value_w_hbm.at[pl.ds(KD, VD - KD)], value_w.at[pl.ds(VD, VD - KD)], load.at[3]),
        pltpu.make_async_copy(query_w_hbm, query_w, load.at[4]),
    ]
    for one in loads:
        one.start()

    barrier = pltpu.get_barrier_semaphore()
    for peer in (x_up, x_down, z_up, z_down, z_far_up, z_far_down, z_three_up, z_three_down, twin, other):
        pl.semaphore_signal(barrier, inc=1, device_id={"seq": peer}, device_id_type=MESH)
    for one in first_loads:
        one.wait()
    pl.semaphore_wait(barrier, 10)

    copies = Copies(send, recv)
    from_before = copies.start(bases_ref, halo.at[0], after)
    from_after = copies.start(bases_ref, halo.at[1], before)

    stem_w[...] = jnp.zeros_like(stem_w)
    for t in range(TAPS):
        stem_w[t * 8 : t * 8 + 4, :] = stem_w_ref[t].astype(F32)
    dev = step_ref[...]
    cos_d, sin_d = dev[:, :KD], dev[:, KD:]
    cos_r, sin_r = rope_ref[:, :KD], rope_ref[:, KD:]
    lane = lax.broadcasted_iota(jnp.int32, (TOK, KD), 1)
    cos = cos_d * cos_r - sin_d * sin_r
    sin = sin_d * cos_r + cos_d * sin_r
    sin = jnp.where(lane < KD // 2, -sin, sin)

    def rotate(u):
        return u * cos + pltpu.roll(u, KD // 2, 1) * sin

    from_before.wait_recv()
    from_after.wait_recv()

    near = [
        jnp.where(me == 0, 0, halo[0, 1:2, :] + 1),
        bases_ref[0:1, :] + 1,
        bases_ref[1:2, :] + 1,
        jnp.where(me == 2 * NX * NZ - 1, 0, halo[1, 0:1, :] + 1),
    ]
    phase = (lax.broadcasted_iota(jnp.int32, (8, 128), 1) & 3) == lax.broadcasted_iota(jnp.int32, (8, 128), 0)
    spot = lax.broadcasted_iota(jnp.int32, (128, 128), 0)
    token = lax.broadcasted_iota(jnp.int32, (128, 128), 1)
    marks = jnp.zeros((8, 128), F32)
    for b in range(4):
        picked = jnp.where(phase, jnp.broadcast_to(near[b], (8, 128)), 0).astype(F32).astype(BF16)
        place = (((spot + (128 * b - 120)) >> 2) == token).astype(F32).astype(BF16)
        marks += jnp.dot(picked, place, preferred_element_type=F32)
    moved = [marks, pltpu.roll(marks, 127, 1), pltpu.roll(marks, 126, 1)]
    base = (lax.broadcasted_iota(jnp.int32, (8, 128), 0) + 1).astype(F32)
    for r in range(4):
        for t in range(TAPS):
            k = r + t - 2
            row = moved[1 + k // 4][k % 4 : k % 4 + 1, :]
            onehot[t * 8 : t * 8 + 8, r * 128 : (r + 1) * 128] = (
                jnp.broadcast_to(row, (8, 128)) == base
            ).astype(F32)
    stem = lax.dot_general(
        onehot[...].astype(BF16), stem_w[...].astype(BF16), (((0,), (0,)), ((), ())),
        preferred_element_type=F32,
    )
    stem = [gelu(stem[r * 128 : r * 128 + 72] + stem_b_ref[...].reshape(1, C1)) for r in range(4)]
    spot = lax.broadcasted_iota(jnp.int32, (72, C1), 0)
    first = jnp.where(me == 0, 1, 0)
    last = jnp.where(me == 2 * NX * NZ - 1, 64, 65)
    inside = (spot >= first) & (spot <= last)
    pooled_e[...] = jnp.where(inside, jnp.maximum(stem[0], stem[1]), 0.0)
    pooled_o[...] = jnp.where(inside, jnp.maximum(stem[2], stem[3]), 0.0)

    shifted = [[ref[pl.ds(o, TOK), :].astype(BF16) for ref in (pooled_e, pooled_o)] for o in range(3)]
    for t in range(TAPS):
        conv_in[0:TOK, t * C1 : (t + 1) * C1] = shifted[t // 2][t % 2]
        conv_in[TOK : 2 * TOK, t * C1 : (t + 1) * C1] = shifted[(t + 1) // 2][(t + 1) % 2]
    loads[0].wait()
    conv = jnp.dot(
        conv_in[...], conv_w[...].reshape(TAPS * C1, C2), preferred_element_type=F32
    ) + conv_b_ref[...].reshape(1, C2)
    conv = gelu(conv)
    features = jnp.maximum(conv[:TOK], conv[TOK:])
    mean_square = jnp.mean(features * features, axis=1, keepdims=True)
    normed = (features * lax.rsqrt(mean_square + 1e-06) * gain_ref[...].reshape(1, C2)).astype(BF16)

    for one in loads[1:4]:
        one.wait()
    keys = rotate(jnp.dot(normed, key_w[...], preferred_element_type=F32)).astype(BF16)
    values = lax.dot_general(normed, value_w[...], (((1,), (1,)), ((), ())), preferred_element_type=F32)
    tails = values[:, KD:]
    values = values[:, :KD].astype(BF16)
    half = lax.broadcasted_iota(jnp.int32, (16, KD), 1) < KD // 2
    for u in range(2):
        buf[0, u, 0:32, :] = keys[u * 32 : u * 32 + 32]
        buf[0, u, 32:64, :] = values[u * 32 : u * 32 + 32]
        buf[0, u, 64:80, :] = jnp.where(
            half, tails[u * 32 : u * 32 + 16], tails[u * 32 + 16 : u * 32 + 32]
        ).astype(BF16)

    def units(d, u, n=1):
        return buf.at[ORDER.index(d), pl.ds(u, n)]

    arrive_a, arrive_b, arrive_x, arrive_o = {}, {}, {}, {}

    def send_a(src, dst, to, u=U_C, n=2):
        arrive_a.setdefault(dst, []).append(copies.start(units(src, u, n), units(dst, u, n), to))

    def send_b(src, dst, to):
        u, n = over_z(dst)
        arrive_b[dst] = [copies.start(units(src, u, n), units(dst, u, n), to)] if n else []

    def send_x(d):
        u, n = over_z(d)
        arrive_x[d] = []
        for side, to in ((U_L, x_up), (U_R, x_down)):
            lacks = [i for i in (0, 1) if not u <= side + i < u + n]
            if lacks:
                src, dst = units(d, U_C + lacks[0], len(lacks)), units(d, side + lacks[0], len(lacks))
                arrive_x[d].append(copies.start(src, dst, to))

    def send_o(d):
        if d == 0:
            sends = ((U_L, U_O, 1, x_up), (U_R + 1, U_O + 1, 1, x_down))
        elif 0 < d < 8:
            sends = ((U_L, U_O, 2, x_up),)
        else:
            sends = ((U_R, U_O, 2, x_down),)
        arrive_o[d] = [copies.start(units(d, u, n), units(d, v, n), to) for u, v, n, to in sends]

    def onward(d, send, needs=lambda dst: True):
        away, back = (z_up, z_down) if d > 0 else (z_down, z_up)
        sign = 1 if d > 0 else -1
        following = [(sign * UP[abs(d)], away)] if abs(d) in UP else []
        following += [(sign * BACK[abs(d)], back)] if abs(d) in BACK else []
        for dst, to in following:
            if needs(dst):
                send(d, dst, to)
        if send is send_a and d == SEED:
            send_a(d, 8, z_three_up, U_C, 1)
        if send is send_a and d == -SEED:
            send_a(d, 8, z_three_down, U_C + 1, 1)

    send_a(0, SEED, z_far_up)
    send_a(0, -SEED, z_far_down)
    send_x(0)
    send_a(0, 1, z_up)
    send_a(0, -1, z_down)

    def take_a(*chunks):
        for d in chunks:
            for copy in arrive_a[d]:
                copy.wait_recv()
            onward(d, send_a)
            send_x(d)

    def take_b(*chunks):
        for d in chunks:
            for copy in arrive_b.get(d, ()):
                copy.wait_recv()
            onward(d, send_b, lambda dst: covers(d, dst))

    def take_x(*chunks):
        for d in chunks:
            for copy in arrive_x[d]:
                copy.wait_recv()
            onward(d, send_b, lambda dst: not covers(d, dst))
            send_o(d)

    loads[4].wait()
    for h in range(HEADS):
        u = jnp.dot(normed, query_w[:, h * KD : (h + 1) * KD], preferred_element_type=F32)
        q_buf[h * TOK : (h + 1) * TOK, :] = rotate(u).astype(BF16)
    queries = copies.start(q_buf.at[pl.ds(0, QROWS)], q_buf.at[pl.ds(QROWS, QROWS)], twin)

    take_x(0)
    send_b(0, SEED, z_far_up)
    send_b(0, -SEED, z_far_down)
    send_b(0, 1, z_up)
    send_b(0, -1, z_down)
    take_a(*STAGES[0])
    acc[...] = jnp.zeros_like(acc)
    tot[...] = jnp.zeros_like(tot)
    queries.wait_recv()

    scale = 1.0 / math.sqrt(KD) / SOFT_CAP
    peak = SOFT_CAP * math.log2(math.e)
    rows, width = 256, 512

    def attend(tile, blocks):
        for d in ORDER[2 * tile : 2 * tile + 2]:
            for copy in arrive_o.pop(d, ()):
                copy.wait_recv()
        key_rows = buf[2 * tile : 2 * tile + 2, :, 0:32, :].reshape(width, KD)
        value_rows = buf[2 * tile : 2 * tile + 2, :, 32:64, :].reshape(width, KD)
        tail = buf[2 * tile : 2 * tile + 2, :, 64:80, :].reshape(width // 32, 16, KD)
        turned = pltpu.roll(tail.astype(F32).reshape(width // 2, KD), KD // 2, 1)
        turned = turned.astype(BF16).reshape(width // 32, 16, KD)
        tail = jnp.concatenate([tail, turned], axis=1).reshape(width, KD)
        right_side = jnp.concatenate([value_rows, tail], axis=1)
        for i in blocks:
            at_rows = pl.ds(i * rows, rows)
            scores = lax.dot_general(
                q_buf[at_rows, :], key_rows, (((1,), (1,)), ((), ())), preferred_element_type=F32
            )
            probability = jnp.exp2(jnp.tanh(scores * scale) * peak - peak)
            tot[at_rows, :] += sum(probability[:, j : j + 128] for j in range(0, width, 128))
            acc[at_rows, :] += jnp.dot(probability.astype(BF16), right_side, preferred_element_type=F32)

    every = range(2 * QROWS // rows)
    tile = 0
    for k in range(1, len(STAGES) + 1):
        if k < len(STAGES):
            take_a(*STAGES[k])
        take_b(*STAGES[k - 1])
        take_x(*STAGES[k - 1])
        known = 1 + sum(len(stage) for stage in STAGES[: k - 1])
        while tile < min(known // 2, 7):
            attend(tile, every)
            tile += 1
    while tile < 7:
        attend(tile, every)
        tile += 1

    wide = lax.broadcasted_iota(jnp.int32, (rows, 2 * KD), 1)
    home = []
    for i in (2, 3):
        attend(7, (i,))
        at_rows = pl.ds(i * rows, rows)
        total = jnp.sum(tot[at_rows, :], axis=1, keepdims=True)
        acc[at_rows, :] = jnp.where(wide < VD, acc[at_rows, :], total)
        home.append(copies.start(acc.at[at_rows], part.at[pl.ds((i - 2) * rows, rows)], twin))
    attend(7, (0, 1))
    for h in range(HEADS):
        if h % 4 == 0:
            home[h // 4].wait_recv()
        at_rows = pl.ds(h * TOK, TOK)
        both = acc[at_rows, :VD] + part[at_rows, :VD]
        total = jnp.sum(tot[at_rows, :], axis=1, keepdims=True) + part[at_rows, VD : VD + 1]
        out_ref[:, h * VD : (h + 1) * VD] = (both * (1.0 / total)).astype(BF16)
    for copy in copies.made:
        copy.wait_send()
    assert len(copies.made) <= N_COPIES


def tables():
    frequency = np.exp(np.arange(KD // 2) * (-2.0 * math.log(ROPE_BASE) / KD))

    def both(places):
        angles = places[:, None] * frequency[None, :]
        return np.concatenate([np.cos(angles)] * 2 + [np.sin(angles)] * 2, axis=1).astype(np.float32)

    return both(np.arange(TOK)), both(np.arange(2 * NX * NZ) * TOK)


def on_device(
    dna_bases, stem_weight, stem_bias, conv_weight, conv_bias, norm_gain, query_weight, key_weight, value_weight
):
    rope, step = tables()
    vmem = pl.BlockSpec(memory_space=pltpu.VMEM)
    anywhere = pl.BlockSpec(memory_space=pltpu.HBM)
    return pl.pallas_call(
        kernel,
        out_shape=jax.ShapeDtypeStruct((TOK, HEADS * VD), BF16),
        in_specs=[anywhere] * 11,
        out_specs=vmem,
        scratch_shapes=[
            pltpu.VMEM((2, 128), jnp.int32),
            pltpu.VMEM((TAPS, 4, C1), BF16),
            pltpu.VMEM((C1,), F32),
            pltpu.VMEM((C2,), F32),
            pltpu.VMEM((C2,), F32),
            pltpu.VMEM((TOK, 2 * KD), F32),
            pltpu.VMEM((1, 2 * KD), F32),
            pltpu.VMEM((2, 2, 128), jnp.int32),
            pltpu.VMEM((40, 512), F32),
            pltpu.VMEM((40, C1), F32),
            pltpu.VMEM((72, C1), F32),
            pltpu.VMEM((72, C1), F32),
            pltpu.VMEM((2 * TOK, TAPS * C1), BF16),
            pltpu.VMEM((TAPS, C1, C2), BF16),
            pltpu.VMEM((C2, HEADS * KD), BF16),
            pltpu.VMEM((C2, KD), BF16),
            pltpu.VMEM((2 * KD, C2), BF16),
            pltpu.VMEM((16, 8, UROWS, 128), BF16),
            pltpu.VMEM((2 * QROWS, KD), BF16),
            pltpu.VMEM((2 * QROWS, 2 * KD), F32),
            pltpu.VMEM((2 * QROWS, 128), F32),
            pltpu.VMEM((QROWS, 2 * KD), F32),
            pltpu.SemaphoreType.DMA((N_COPIES,)),
            pltpu.SemaphoreType.DMA((N_COPIES,)),
            pltpu.SemaphoreType.DMA((13,)),
        ],
        compiler_params=pltpu.CompilerParams(
            collective_id=0, has_side_effects=True, vmem_limit_bytes=44 << 20
        ),
    )(*(
        pltpu.with_memory_space_constraint(one, pltpu.HBM)
        for one in (
            dna_bases, stem_weight, stem_bias, conv_bias, norm_gain, jnp.asarray(rope), jnp.asarray(step),
            conv_weight, query_weight, key_weight, value_weight.T,
        )
    ))


def solution(mesh):
    placed = (P(("batch", "seq")), P(), P(), P(), P(), P(), P(), P(), P())
    return jax.shard_map(
        on_device, mesh=mesh, in_specs=placed, out_specs=P(("batch", "seq"), None), check_vma=False
    )
```

```python
import functools
import math

import jax
import jax.numpy as jnp
import numpy as np
from jax import lax
from jax.experimental import pallas as pl
from jax.experimental.pallas import tpu as pltpu
from jax.sharding import PartitionSpec as P

MESH = pl.DeviceIdType.MESH
SOFT_CAP = 20.0
ROPE_BASE = 10000.0
NX, NZ = 4, 16
TOK = 64
C1, C2, HEADS, KD, VD, TAPS = 384, 768, 8, 128, 192, 5
UROWS = 80
QROWS = TOK * HEADS
F32, BF16 = jnp.float32, jnp.bfloat16

U_C, U_L, U_R, U_O = 0, 2, 4, 6

ORDER = (0, 1, -1, 5, -5, 2, -2, 6, -6, 4, -4, 7, -7, 3, -3, 8)
OVER_Z = {1: 2, -1: 2, 2: 2, -2: 2, 5: 2, -5: 2, 6: 4, -6: 4, 4: 4, -4: 4, 7: 4, -7: 4, 3: 4, -3: 4, 8: 2}
SEED = 5
STAGES = ((1, -1), (5, -5, 2, -2), (6, -6, 4, -4), (7, -7, 3, -3, 8))
UP, BACK = {1: 2, 5: 6, 6: 7}, {5: 4, 4: 3}


def over_z(d):
    ahead = 0 < d < 8
    return {
        2: (U_L, 0), 3: (U_L + 1, 1) if ahead else (U_R, 1), 4: (U_L + 1, 2), 5: (U_L, 3) if ahead else (U_L + 1, 3)
    }[OVER_Z.get(d, 2)]


def covers(src, dst):
    (u, n), (v, m) = over_z(src), over_z(dst)
    return src != 0 and u <= v and v + m <= u + n


def gelu(x):
    inner = math.sqrt(2.0 / math.pi) * (x + 0.044715 * (x * x * x))
    return (0.5 * x) * (1.0 + jnp.tanh(inner))


class Copies:
    def __init__(self, send, recv):
        self.send, self.recv, self.made = send, recv, []

    def start(self, src, dst, to):
        k = len(self.made)
        copy = pltpu.make_async_remote_copy(
            src_ref=src, dst_ref=dst, send_sem=self.send.at[k], recv_sem=self.recv.at[k],
            device_id={"seq": to}, device_id_type=MESH,
        )
        copy.start()
        self.made.append(copy)
        return copy


N_COPIES = 96


def kernel(
    bases_hbm, stem_w_hbm, stem_b_hbm, conv_b_hbm, gain_hbm, rope_hbm, step_hbm,
    conv_w_hbm, query_w_hbm, key_w_hbm, value_w_hbm,
    out_ref,
    bases_ref, stem_w_ref, stem_b_ref, conv_b_ref, gain_ref, rope_ref, step_ref,
    halo, onehot, stem_w, pooled_e, pooled_o, conv_in, conv_w, query_w, key_w, value_w,
    buf, q_buf, acc, tot, part, send, recv, load,
):
    me = lax.axis_index("seq")
    core, z, x = me % 2, (me // 2) % NZ, me // (2 * NZ)

    def at(xx, zz, cc):
        return ((xx % NX) * NZ + zz % NZ) * 2 + cc

    x_up, x_down = at(x + 1, z, core), at(x + NX - 1, z, core)
    z_up, z_down = at(x, z + 1, core), at(x, z + NZ - 1, core)
    z_far_up, z_far_down = at(x, z + SEED, core), at(x, z + NZ - SEED, core)
    z_three_up, z_three_down = at(x, z + 8 - SEED, core), at(x, z + NZ - 8 + SEED, core)
    twin = at(x, z, 1 - core)
    after, before = (me + 1) % (2 * NX * NZ), (me + 2 * NX * NZ - 1) % (2 * NX * NZ)
    other = jnp.where(core == 0, before, after)

    first_loads = [
        pltpu.make_async_copy(bases_hbm.at[pl.ds(0, 128)], bases_ref.at[0], load.at[5]),
        pltpu.make_async_copy(bases_hbm.at[pl.ds(128, 128)], bases_ref.at[1], load.at[6]),
        pltpu.make_async_copy(stem_w_hbm, stem_w_ref, load.at[7]),
        pltpu.make_async_copy(stem_b_hbm, stem_b_ref, load.at[8]),
        pltpu.make_async_copy(rope_hbm, rope_ref, load.at[9]),
        pltpu.make_async_copy(step_hbm.at[pl.ds(me, 1)], step_ref, load.at[10]),
        pltpu.make_async_copy(conv_b_hbm, conv_b_ref, load.at[11]),
        pltpu.make_async_copy(gain_hbm, gain_ref, load.at[12]),
    ]
    for one in first_loads:
        one.start()
    loads = [
        pltpu.make_async_copy(conv_w_hbm, conv_w, load.at[0]),
        pltpu.make_async_copy(key_w_hbm, key_w, load.at[1]),
        pltpu.make_async_copy(value_w_hbm, value_w.at[pl.ds(0, VD)], load.at[2]),
        pltpu.make_async_copy(value_w_hbm.at[pl.ds(KD, VD - KD)], value_w.at[pl.ds(VD, VD - KD)], load.at[3]),
        pltpu.make_async_copy(query_w_hbm, query_w, load.at[4]),
    ]
    for one in loads:
        one.start()

    barrier = pltpu.get_barrier_semaphore()
    for peer in (x_up, x_down, z_up, z_down, z_far_up, z_far_down, z_three_up, z_three_down, twin, other):
        pl.semaphore_signal(barrier, inc=1, device_id={"seq": peer}, device_id_type=MESH)
    for one in first_loads:
        one.wait()
    pl.semaphore_wait(barrier, 10)

    copies = Copies(send, recv)
    from_before = copies.start(bases_ref, halo.at[0], after)
    from_after = copies.start(bases_ref, halo.at[1], before)

    stem_w[...] = jnp.zeros_like(stem_w)
    for t in range(TAPS):
        stem_w[t * 8 : t * 8 + 4, :] = stem_w_ref[t].astype(F32)
    dev = step_ref[...]
    cos_d, sin_d = dev[:, :KD], dev[:, KD:]
    cos_r, sin_r = rope_ref[:, :KD], rope_ref[:, KD:]
    lane = lax.broadcasted_iota(jnp.int32, (TOK, KD), 1)
    cos = cos_d * cos_r - sin_d * sin_r
    sin = sin_d * cos_r + cos_d * sin_r
    sin = jnp.where(lane < KD // 2, -sin, sin)

    def rotate(u):
        return u * cos + pltpu.roll(u, KD // 2, 1) * sin

    from_before.wait_recv()
    from_after.wait_recv()

    near = [
        jnp.where(me == 0, 0, halo[0, 1:2, :] + 1),
        bases_ref[0:1, :] + 1,
        bases_ref[1:2, :] + 1,
        jnp.where(me == 2 * NX * NZ - 1, 0, halo[1, 0:1, :] + 1),
    ]
    phase = (lax.broadcasted_iota(jnp.int32, (8, 128), 1) & 3) == lax.broadcasted_iota(jnp.int32, (8, 128), 0)
    spot = lax.broadcasted_iota(jnp.int32, (128, 128), 0)
    token = lax.broadcasted_iota(jnp.int32, (128, 128), 1)
    marks = jnp.zeros((8, 128), F32)
    for b in range(4):
        picked = jnp.where(phase, jnp.broadcast_to(near[b], (8, 128)), 0).astype(F32).astype(BF16)
        place = (((spot + (128 * b - 120)) >> 2) == token).astype(F32).astype(BF16)
        marks += jnp.dot(picked, place, preferred_element_type=F32)
    moved = [marks, pltpu.roll(marks, 127, 1), pltpu.roll(marks, 126, 1)]
    base = (lax.broadcasted_iota(jnp.int32, (8, 128), 0) + 1).astype(F32)
    for r in range(4):
        for t in range(TAPS):
            k = r + t - 2
            row = moved[1 + k // 4][k % 4 : k % 4 + 1, :]
            onehot[t * 8 : t * 8 + 8, r * 128 : (r + 1) * 128] = (
                jnp.broadcast_to(row, (8, 128)) == base
            ).astype(F32)
    stem = lax.dot_general(
        onehot[...].astype(BF16), stem_w[...].astype(BF16), (((0,), (0,)), ((), ())),
        preferred_element_type=F32,
    )
    stem = [gelu(stem[r * 128 : r * 128 + 72] + stem_b_ref[...].reshape(1, C1)) for r in range(4)]
    spot = lax.broadcasted_iota(jnp.int32, (72, C1), 0)
    first = jnp.where(me == 0, 1, 0)
    last = jnp.where(me == 2 * NX * NZ - 1, 64, 65)
    inside = (spot >= first) & (spot <= last)
    pooled_e[...] = jnp.where(inside, jnp.maximum(stem[0], stem[1]), 0.0)
    pooled_o[...] = jnp.where(inside, jnp.maximum(stem[2], stem[3]), 0.0)

    shifted = [[ref[pl.ds(o, TOK), :].astype(BF16) for ref in (pooled_e, pooled_o)] for o in range(3)]
    for t in range(TAPS):
        conv_in[0:TOK, t * C1 : (t + 1) * C1] = shifted[t // 2][t % 2]
        conv_in[TOK : 2 * TOK, t * C1 : (t + 1) * C1] = shifted[(t + 1) // 2][(t + 1) % 2]
    loads[0].wait()
    conv = jnp.dot(
        conv_in[...], conv_w[...].reshape(TAPS * C1, C2), preferred_element_type=F32
    ) + conv_b_ref[...].reshape(1, C2)
    conv = gelu(conv)
    features = jnp.maximum(conv[:TOK], conv[TOK:])
    mean_square = jnp.mean(features * features, axis=1, keepdims=True)
    normed = (features * lax.rsqrt(mean_square + 1e-06) * gain_ref[...].reshape(1, C2)).astype(BF16)

    for one in loads[1:4]:
        one.wait()
    keys = rotate(jnp.dot(normed, key_w[...], preferred_element_type=F32)).astype(BF16)
    values = lax.dot_general(normed, value_w[...], (((1,), (1,)), ((), ())), preferred_element_type=F32)
    tails = values[:, KD:]
    values = values[:, :KD].astype(BF16)
    half = lax.broadcasted_iota(jnp.int32, (16, KD), 1) < KD // 2
    for u in range(2):
        buf[0, u, 0:32, :] = keys[u * 32 : u * 32 + 32]
        buf[0, u, 32:64, :] = values[u * 32 : u * 32 + 32]
        buf[0, u, 64:80, :] = jnp.where(
            half, tails[u * 32 : u * 32 + 16], tails[u * 32 + 16 : u * 32 + 32]
        ).astype(BF16)

    def units(d, u, n=1):
        return buf.at[ORDER.index(d), pl.ds(u, n)]

    arrive_a, arrive_b, arrive_x, arrive_o = {}, {}, {}, {}

    def send_a(src, dst, to, u=U_C, n=2):
        arrive_a.setdefault(dst, []).append(copies.start(units(src, u, n), units(dst, u, n), to))

    def send_b(src, dst, to):
        u, n = over_z(dst)
        arrive_b[dst] = [copies.start(units(src, u, n), units(dst, u, n), to)] if n else []

    def send_x(d):
        u, n = over_z(d)
        arrive_x[d] = []
        for side, to in ((U_L, x_up), (U_R, x_down)):
            lacks = [i for i in (0, 1) if not u <= side + i < u + n]
            if lacks:
                src, dst = units(d, U_C + lacks[0], len(lacks)), units(d, side + lacks[0], len(lacks))
                arrive_x[d].append(copies.start(src, dst, to))

    def send_o(d):
        if d == 0:
            sends = ((U_L, U_O, 1, x_up), (U_R + 1, U_O + 1, 1, x_down))
        elif 0 < d < 8:
            sends = ((U_L, U_O, 2, x_up),)
        else:
            sends = ((U_R, U_O, 2, x_down),)
        arrive_o[d] = [copies.start(units(d, u, n), units(d, v, n), to) for u, v, n, to in sends]

    def onward(d, send, needs=lambda dst: True):
        away, back = (z_up, z_down) if d > 0 else (z_down, z_up)
        sign = 1 if d > 0 else -1
        following = [(sign * UP[abs(d)], away)] if abs(d) in UP else []
        following += [(sign * BACK[abs(d)], back)] if abs(d) in BACK else []
        for dst, to in following:
            if needs(dst):
                send(d, dst, to)
        if send is send_a and d == SEED:
            send_a(d, 8, z_three_up, U_C, 1)
        if send is send_a and d == -SEED:
            send_a(d, 8, z_three_down, U_C + 1, 1)

    send_a(0, SEED, z_far_up)
    send_a(0, -SEED, z_far_down)
    send_x(0)
    send_a(0, 1, z_up)
    send_a(0, -1, z_down)

    def take_a(*chunks):
        for d in chunks:
            for copy in arrive_a[d]:
                copy.wait_recv()
            onward(d, send_a)
            send_x(d)

    def take_b(*chunks):
        for d in chunks:
            for copy in arrive_b.get(d, ()):
                copy.wait_recv()
            onward(d, send_b, lambda dst: covers(d, dst))

    def take_x(*chunks):
        for d in chunks:
            for copy in arrive_x[d]:
                copy.wait_recv()
            onward(d, send_b, lambda dst: not covers(d, dst))
            send_o(d)

    loads[4].wait()
    for h in range(HEADS):
        u = jnp.dot(normed, query_w[:, h * KD : (h + 1) * KD], preferred_element_type=F32)
        q_buf[h * TOK : (h + 1) * TOK, :] = rotate(u).astype(BF16)
    queries = copies.start(q_buf.at[pl.ds(0, QROWS)], q_buf.at[pl.ds(QROWS, QROWS)], twin)

    take_x(0)
    send_b(0, SEED, z_far_up)
    send_b(0, -SEED, z_far_down)
    send_b(0, 1, z_up)
    send_b(0, -1, z_down)
    take_a(*STAGES[0])
    acc[...] = jnp.zeros_like(acc)
    tot[...] = jnp.zeros_like(tot)
    queries.wait_recv()

    scale = 1.0 / math.sqrt(KD) / SOFT_CAP
    peak = SOFT_CAP * math.log2(math.e)
    rows = 256

    def attend(chunks, first_unit, n_units, blocks):
        if first_unit + n_units == 8:
            for d in chunks:
                for copy in arrive_o.pop(d, ()):
                    copy.wait_recv()
        start, n = ORDER.index(chunks[0]), len(chunks)
        width = n * n_units * 32

        def part_of(low, high):
            piece = buf[start : start + n, first_unit : first_unit + n_units, low:high, :]
            return piece.reshape(n * n_units, high - low, KD)

        key_rows = part_of(0, 32).reshape(width, KD)
        value_rows = part_of(32, 64).reshape(width, KD)
        tail = part_of(64, 80)
        turned = pltpu.roll(tail.astype(F32).reshape(width // 2, KD), KD // 2, 1)
        turned = turned.astype(BF16).reshape(n * n_units, 16, KD)
        tail = jnp.concatenate([tail, turned], axis=1).reshape(width, KD)
        right_side = jnp.concatenate([value_rows, tail], axis=1)
        for i in blocks:
            at_rows = pl.ds(i * rows, rows)
            scores = lax.dot_general(
                q_buf[at_rows, :], key_rows, (((1,), (1,)), ((), ())), preferred_element_type=F32
            )
            probability = jnp.exp2(jnp.tanh(scores * scale) * peak - peak)
            tot[at_rows, :] += sum(probability[:, j : j + 128] for j in range(0, width - 127, 128))
            if width % 128:
                tot[at_rows, : width % 128] += probability[:, width - width % 128 :]
            acc[at_rows, :] += jnp.dot(probability.astype(BF16), right_side, preferred_element_type=F32)

    every = range(2 * QROWS // rows)
    for k in range(1, len(STAGES) + 1):
        if k < len(STAGES):
            take_a(*STAGES[k])
        take_b(*STAGES[k - 1])
        take_x(*STAGES[k - 1])
        if k == 2:
            attend((0,) + STAGES[0], 0, 8, every)
        if k == 3:
            attend(STAGES[1], 0, 8, every)
            attend(STAGES[2], 0, 6, every)
        if k == 4:
            attend(STAGES[2], 6, 2, every)
            attend(STAGES[3], 0, 6, every)

    wide = lax.broadcasted_iota(jnp.int32, (rows, 2 * KD), 1)
    home = []
    for i in (2, 3):
        attend(STAGES[3], 6, 2, (i,))
        at_rows = pl.ds(i * rows, rows)
        total = jnp.sum(tot[at_rows, :], axis=1, keepdims=True)
        acc[at_rows, :] = jnp.where(wide < VD, acc[at_rows, :], total)
        home.append(copies.start(acc.at[at_rows], part.at[pl.ds((i - 2) * rows, rows)], twin))
    attend(STAGES[3], 6, 2, (0, 1))
    for h in range(HEADS):
        if h % 4 == 0:
            home[h // 4].wait_recv()
        at_rows = pl.ds(h * TOK, TOK)
        both = acc[at_rows, :VD] + part[at_rows, :VD]
        total = jnp.sum(tot[at_rows, :], axis=1, keepdims=True) + part[at_rows, VD : VD + 1]
        out_ref[:, h * VD : (h + 1) * VD] = (both * (1.0 / total)).astype(BF16)
    for copy in copies.made:
        copy.wait_send()
    assert len(copies.made) <= N_COPIES


def tables():
    frequency = np.exp(np.arange(KD // 2) * (-2.0 * math.log(ROPE_BASE) / KD))

    def both(places):
        angles = places[:, None] * frequency[None, :]
        return np.concatenate([np.cos(angles)] * 2 + [np.sin(angles)] * 2, axis=1).astype(np.float32)

    return both(np.arange(TOK)), both(np.arange(2 * NX * NZ) * TOK)


def on_device(
    dna_bases, stem_weight, stem_bias, conv_weight, conv_bias, norm_gain, query_weight, key_weight, value_weight
):
    rope, step = tables()
    vmem = pl.BlockSpec(memory_space=pltpu.VMEM)
    anywhere = pl.BlockSpec(memory_space=pltpu.HBM)
    return pl.pallas_call(
        kernel,
        out_shape=jax.ShapeDtypeStruct((TOK, HEADS * VD), BF16),
        in_specs=[anywhere] * 11,
        out_specs=vmem,
        scratch_shapes=[
            pltpu.VMEM((2, 128), jnp.int32),
            pltpu.VMEM((TAPS, 4, C1), BF16),
            pltpu.VMEM((C1,), F32),
            pltpu.VMEM((C2,), F32),
            pltpu.VMEM((C2,), F32),
            pltpu.VMEM((TOK, 2 * KD), F32),
            pltpu.VMEM((1, 2 * KD), F32),
            pltpu.VMEM((2, 2, 128), jnp.int32),
            pltpu.VMEM((40, 512), F32),
            pltpu.VMEM((40, C1), F32),
            pltpu.VMEM((72, C1), F32),
            pltpu.VMEM((72, C1), F32),
            pltpu.VMEM((2 * TOK, TAPS * C1), BF16),
            pltpu.VMEM((TAPS, C1, C2), BF16),
            pltpu.VMEM((C2, HEADS * KD), BF16),
            pltpu.VMEM((C2, KD), BF16),
            pltpu.VMEM((2 * KD, C2), BF16),
            pltpu.VMEM((16, 8, UROWS, 128), BF16),
            pltpu.VMEM((2 * QROWS, KD), BF16),
            pltpu.VMEM((2 * QROWS, 2 * KD), F32),
            pltpu.VMEM((2 * QROWS, 128), F32),
            pltpu.VMEM((QROWS, 2 * KD), F32),
            pltpu.SemaphoreType.DMA((N_COPIES,)),
            pltpu.SemaphoreType.DMA((N_COPIES,)),
            pltpu.SemaphoreType.DMA((13,)),
        ],
        compiler_params=pltpu.CompilerParams(
            collective_id=0, has_side_effects=True, vmem_limit_bytes=44 << 20
        ),
    )(*(
        pltpu.with_memory_space_constraint(one, pltpu.HBM)
        for one in (
            dna_bases, stem_weight, stem_bias, conv_bias, norm_gain, jnp.asarray(rope), jnp.asarray(step),
            conv_weight, query_weight, key_weight, value_weight.T,
        )
    ))


def solution(mesh):
    placed = (P(("batch", "seq")), P(), P(), P(), P(), P(), P(), P(), P())
    return jax.shard_map(
        on_device, mesh=mesh, in_specs=placed, out_specs=P(("batch", "seq"), None), check_vma=False
    )
```

```python
import functools
import math

import jax
import jax.numpy as jnp
import numpy as np
from jax import lax
from jax.experimental import pallas as pl
from jax.experimental.pallas import tpu as pltpu
from jax.sharding import PartitionSpec as P

MESH = pl.DeviceIdType.MESH
SOFT_CAP = 20.0
ROPE_BASE = 10000.0
NX, NZ = 4, 16
TOK = 64
C1, C2, HEADS, KD, VD, TAPS = 384, 768, 8, 128, 192, 5
UROWS = 80
QROWS = TOK * HEADS
F32, BF16 = jnp.float32, jnp.bfloat16

U_C, U_L, U_R, U_O = 0, 2, 4, 6

ORDER = (0, 1, -1, 5, -5, 2, -2, 6, -6, 4, -4, 7, -7, 3, -3, 8)
OVER_Z = {1: 2, -1: 2, 2: 2, -2: 2, 5: 2, -5: 2, 6: 4, -6: 4, 4: 4, -4: 4, 7: 4, -7: 4, 3: 4, -3: 4, 8: 2}
SEED = 5
STAGES = ((1, -1), (5, -5, 2, -2), (6, -6, 4, -4), (7, -7, 3, -3, 8))
UP, BACK = {1: 2, 5: 6, 6: 7}, {5: 4, 4: 3}


def over_z(d):
    ahead = 0 < d < 8
    return {
        2: (U_L, 0), 3: (U_L + 1, 1) if ahead else (U_R, 1), 4: (U_L + 1, 2), 5: (U_L, 3) if ahead else (U_L + 1, 3)
    }[OVER_Z.get(d, 2)]


def covers(src, dst):
    (u, n), (v, m) = over_z(src), over_z(dst)
    return src != 0 and u <= v and v + m <= u + n


def gelu(x):
    inner = math.sqrt(2.0 / math.pi) * (x + 0.044715 * (x * x * x))
    return (0.5 * x) * (1.0 + jnp.tanh(inner))


class Copies:
    def __init__(self, send, recv):
        self.send, self.recv, self.made = send, recv, []

    def start(self, src, dst, to):
        k = len(self.made)
        copy = pltpu.make_async_remote_copy(
            src_ref=src, dst_ref=dst, send_sem=self.send.at[k], recv_sem=self.recv.at[k],
            device_id={"seq": to}, device_id_type=MESH,
        )
        copy.start()
        self.made.append(copy)
        return copy


N_COPIES = 96


def kernel(
    bases_hbm, stem_w_hbm, stem_b_hbm, conv_b_hbm, gain_hbm, rope_hbm, step_hbm,
    conv_w_hbm, query_w_hbm, key_w_hbm, value_w_hbm,
    out_ref,
    bases_ref, stem_w_ref, stem_b_ref, conv_b_ref, gain_ref, rope_ref, step_ref,
    halo, onehot, stem_w, pooled_e, pooled_o, conv_in, conv_w, query_w, key_w, value_w,
    buf, q_buf, acc, tot, part, send, recv, load,
):
    me = lax.axis_index("seq")
    core, z, x = me % 2, (me // 2) % NZ, me // (2 * NZ)

    def at(xx, zz, cc):
        return ((xx % NX) * NZ + zz % NZ) * 2 + cc

    x_up, x_down = at(x + 1, z, core), at(x + NX - 1, z, core)
    z_up, z_down = at(x, z + 1, core), at(x, z + NZ - 1, core)
    z_far_up, z_far_down = at(x, z + SEED, core), at(x, z + NZ - SEED, core)
    z_three_up, z_three_down = at(x, z + 8 - SEED, core), at(x, z + NZ - 8 + SEED, core)
    twin = at(x, z, 1 - core)
    after, before = (me + 1) % (2 * NX * NZ), (me + 2 * NX * NZ - 1) % (2 * NX * NZ)
    other = jnp.where(core == 0, before, after)

    first_loads = [
        pltpu.make_async_copy(bases_hbm.at[pl.ds(0, 128)], bases_ref.at[0], load.at[5]),
        pltpu.make_async_copy(bases_hbm.at[pl.ds(128, 128)], bases_ref.at[1], load.at[6]),
        pltpu.make_async_copy(stem_w_hbm, stem_w_ref, load.at[7]),
        pltpu.make_async_copy(stem_b_hbm, stem_b_ref, load.at[8]),
        pltpu.make_async_copy(rope_hbm, rope_ref, load.at[9]),
        pltpu.make_async_copy(step_hbm.at[pl.ds(me, 1)], step_ref, load.at[10]),
        pltpu.make_async_copy(conv_b_hbm, conv_b_ref, load.at[11]),
        pltpu.make_async_copy(gain_hbm, gain_ref, load.at[12]),
    ]
    for one in first_loads:
        one.start()
    loads = [
        pltpu.make_async_copy(conv_w_hbm, conv_w, load.at[0]),
        pltpu.make_async_copy(key_w_hbm, key_w, load.at[1]),
        pltpu.make_async_copy(value_w_hbm, value_w.at[pl.ds(0, VD)], load.at[2]),
        pltpu.make_async_copy(value_w_hbm.at[pl.ds(KD, VD - KD)], value_w.at[pl.ds(VD, VD - KD)], load.at[3]),
        pltpu.make_async_copy(query_w_hbm, query_w, load.at[4]),
    ]
    for one in loads:
        one.start()

    barrier = pltpu.get_barrier_semaphore()
    for peer in (x_up, x_down, z_up, z_down, z_far_up, z_far_down, z_three_up, z_three_down, twin, other):
        pl.semaphore_signal(barrier, inc=1, device_id={"seq": peer}, device_id_type=MESH)
    for one in first_loads[:2]:
        one.wait()
    pl.semaphore_wait(barrier, 10)

    copies = Copies(send, recv)
    from_before = copies.start(bases_ref, halo.at[0], after)
    from_after = copies.start(bases_ref, halo.at[1], before)

    for one in first_loads[2:]:
        one.wait()
    stem_w[...] = jnp.zeros_like(stem_w)
    for t in range(TAPS):
        stem_w[t * 8 : t * 8 + 4, :] = stem_w_ref[t].astype(F32)
    dev = step_ref[...]
    cos_d, sin_d = dev[:, :KD], dev[:, KD:]
    cos_r, sin_r = rope_ref[:, :KD], rope_ref[:, KD:]
    lane = lax.broadcasted_iota(jnp.int32, (TOK, KD), 1)
    cos = cos_d * cos_r - sin_d * sin_r
    sin = sin_d * cos_r + cos_d * sin_r
    sin = jnp.where(lane < KD // 2, -sin, sin)

    def rotate(u):
        return u * cos + pltpu.roll(u, KD // 2, 1) * sin

    from_before.wait_recv()
    from_after.wait_recv()

    near = [
        jnp.where(me == 0, 0, halo[0, 1:2, :] + 1),
        bases_ref[0:1, :] + 1,
        bases_ref[1:2, :] + 1,
        jnp.where(me == 2 * NX * NZ - 1, 0, halo[1, 0:1, :] + 1),
    ]
    phase = (lax.broadcasted_iota(jnp.int32, (8, 128), 1) & 3) == lax.broadcasted_iota(jnp.int32, (8, 128), 0)
    spot = lax.broadcasted_iota(jnp.int32, (128, 128), 0)
    token = lax.broadcasted_iota(jnp.int32, (128, 128), 1)
    marks = jnp.zeros((8, 128), F32)
    for b in range(4):
        picked = jnp.where(phase, jnp.broadcast_to(near[b], (8, 128)), 0).astype(F32).astype(BF16)
        place = (((spot + (128 * b - 120)) >> 2) == token).astype(F32).astype(BF16)
        marks += jnp.dot(picked, place, preferred_element_type=F32)
    moved = [marks, pltpu.roll(marks, 127, 1), pltpu.roll(marks, 126, 1)]
    base = (lax.broadcasted_iota(jnp.int32, (8, 128), 0) + 1).astype(F32)
    for r in range(4):
        for t in range(TAPS):
            k = r + t - 2
            row = moved[1 + k // 4][k % 4 : k % 4 + 1, :]
            onehot[t * 8 : t * 8 + 8, r * 128 : (r + 1) * 128] = (
                jnp.broadcast_to(row, (8, 128)) == base
            ).astype(F32)
    stem = lax.dot_general(
        onehot[...].astype(BF16), stem_w[...].astype(BF16), (((0,), (0,)), ((), ())),
        preferred_element_type=F32,
    )
    stem = [gelu(stem[r * 128 : r * 128 + 72] + stem_b_ref[...].reshape(1, C1)) for r in range(4)]
    spot = lax.broadcasted_iota(jnp.int32, (72, C1), 0)
    first = jnp.where(me == 0, 1, 0)
    last = jnp.where(me == 2 * NX * NZ - 1, 64, 65)
    inside = (spot >= first) & (spot <= last)
    pooled_e[...] = jnp.where(inside, jnp.maximum(stem[0], stem[1]), 0.0)
    pooled_o[...] = jnp.where(inside, jnp.maximum(stem[2], stem[3]), 0.0)

    shifted = [[ref[pl.ds(o, TOK), :].astype(BF16) for ref in (pooled_e, pooled_o)] for o in range(3)]
    for t in range(TAPS):
        conv_in[0:TOK, t * C1 : (t + 1) * C1] = shifted[t // 2][t % 2]
        conv_in[TOK : 2 * TOK, t * C1 : (t + 1) * C1] = shifted[(t + 1) // 2][(t + 1) % 2]
    loads[0].wait()
    conv = jnp.dot(
        conv_in[...], conv_w[...].reshape(TAPS * C1, C2), preferred_element_type=F32
    ) + conv_b_ref[...].reshape(1, C2)
    conv = gelu(conv)
    features = jnp.maximum(conv[:TOK], conv[TOK:])
    mean_square = jnp.mean(features * features, axis=1, keepdims=True)
    normed = (features * lax.rsqrt(mean_square + 1e-06) * gain_ref[...].reshape(1, C2)).astype(BF16)

    for one in loads[1:4]:
        one.wait()
    keys = rotate(jnp.dot(normed, key_w[...], preferred_element_type=F32)).astype(BF16)
    values = lax.dot_general(normed, value_w[...], (((1,), (1,)), ((), ())), preferred_element_type=F32)
    tails = values[:, KD:]
    values = values[:, :KD].astype(BF16)
    half = lax.broadcasted_iota(jnp.int32, (16, KD), 1) < KD // 2
    for u in range(2):
        buf[0, u, 0:32, :] = keys[u * 32 : u * 32 + 32]
        buf[0, u, 32:64, :] = values[u * 32 : u * 32 + 32]
        buf[0, u, 64:80, :] = jnp.where(
            half, tails[u * 32 : u * 32 + 16], tails[u * 32 + 16 : u * 32 + 32]
        ).astype(BF16)

    def units(d, u, n=1):
        return buf.at[ORDER.index(d), pl.ds(u, n)]

    arrive_a, arrive_b, arrive_x, arrive_o = {}, {}, {}, {}

    def send_a(src, dst, to, u=U_C, n=2):
        arrive_a.setdefault(dst, []).append(copies.start(units(src, u, n), units(dst, u, n), to))

    def send_b(src, dst, to):
        u, n = over_z(dst)
        arrive_b[dst] = [copies.start(units(src, u, n), units(dst, u, n), to)] if n else []

    def send_x(d):
        u, n = over_z(d)
        arrive_x[d] = []
        for side, to in ((U_L, x_up), (U_R, x_down)):
            lacks = [i for i in (0, 1) if not u <= side + i < u + n]
            if lacks:
                src, dst = units(d, U_C + lacks[0], len(lacks)), units(d, side + lacks[0], len(lacks))
                arrive_x[d].append(copies.start(src, dst, to))

    def send_o(d):
        if d == 0:
            sends = ((U_L, U_O, 1, x_up), (U_R + 1, U_O + 1, 1, x_down))
        elif 0 < d < 8:
            sends = ((U_L, U_O, 2, x_up),)
        else:
            sends = ((U_R, U_O, 2, x_down),)
        arrive_o[d] = [copies.start(units(d, u, n), units(d, v, n), to) for u, v, n, to in sends]

    def onward(d, send, needs=lambda dst: True):
        away, back = (z_up, z_down) if d > 0 else (z_down, z_up)
        sign = 1 if d > 0 else -1
        following = [(sign * UP[abs(d)], away)] if abs(d) in UP else []
        following += [(sign * BACK[abs(d)], back)] if abs(d) in BACK else []
        for dst, to in following:
            if needs(dst):
                send(d, dst, to)
        if send is send_a and d == SEED:
            send_a(d, 8, z_three_up, U_C, 1)
        if send is send_a and d == -SEED:
            send_a(d, 8, z_three_down, U_C + 1, 1)

    send_a(0, SEED, z_far_up)
    send_a(0, -SEED, z_far_down)
    send_x(0)
    send_a(0, 1, z_up)
    send_a(0, -1, z_down)

    def take_a(*chunks):
        for d in chunks:
            for copy in arrive_a[d]:
                copy.wait_recv()
            onward(d, send_a)
            send_x(d)

    def take_b(*chunks):
        for d in chunks:
            for copy in arrive_b.get(d, ()):
                copy.wait_recv()
            onward(d, send_b, lambda dst: covers(d, dst))

    def take_x(*chunks):
        for d in chunks:
            for copy in arrive_x[d]:
                copy.wait_recv()
            onward(d, send_b, lambda dst: not covers(d, dst))
            send_o(d)

    loads[4].wait()
    for h in range(HEADS):
        u = jnp.dot(normed, query_w[:, h * KD : (h + 1) * KD], preferred_element_type=F32)
        q_buf[h * TOK : (h + 1) * TOK, :] = rotate(u).astype(BF16)
    queries = copies.start(q_buf.at[pl.ds(0, QROWS)], q_buf.at[pl.ds(QROWS, QROWS)], twin)

    take_x(0)
    send_b(0, SEED, z_far_up)
    send_b(0, -SEED, z_far_down)
    send_b(0, 1, z_up)
    send_b(0, -1, z_down)
    take_a(*STAGES[0])
    acc[...] = jnp.zeros_like(acc)
    tot[...] = jnp.zeros_like(tot)
    queries.wait_recv()

    scale = 1.0 / math.sqrt(KD) / SOFT_CAP
    peak = SOFT_CAP * math.log2(math.e)
    rows = 256

    def attend(chunks, first_unit, n_units, blocks):
        if first_unit + n_units == 8:
            for d in chunks:
                for copy in arrive_o.pop(d, ()):
                    copy.wait_recv()
        start, n = ORDER.index(chunks[0]), len(chunks)
        width = n * n_units * 32

        def part_of(low, high):
            piece = buf[start : start + n, first_unit : first_unit + n_units, low:high, :]
            return piece.reshape(n * n_units, high - low, KD)

        key_rows = part_of(0, 32).reshape(width, KD)
        value_rows = part_of(32, 64).reshape(width, KD)
        tail = part_of(64, 80)
        turned = pltpu.roll(tail.astype(F32).reshape(width // 2, KD), KD // 2, 1)
        turned = turned.astype(BF16).reshape(n * n_units, 16, KD)
        tail = jnp.concatenate([tail, turned], axis=1).reshape(width, KD)
        right_side = jnp.concatenate([value_rows, tail], axis=1)
        for i in blocks:
            at_rows = pl.ds(i * rows, rows)
            scores = lax.dot_general(
                q_buf[at_rows, :], key_rows, (((1,), (1,)), ((), ())), preferred_element_type=F32
            )
            probability = jnp.exp2(jnp.tanh(scores * scale) * peak - peak)
            tot[at_rows, :] += sum(probability[:, j : j + 128] for j in range(0, width - 127, 128))
            if width % 128:
                tot[at_rows, : width % 128] += probability[:, width - width % 128 :]
            acc[at_rows, :] += jnp.dot(probability.astype(BF16), right_side, preferred_element_type=F32)

    every = range(2 * QROWS // rows)
    for k in range(1, len(STAGES) + 1):
        if k < len(STAGES):
            take_a(*STAGES[k])
        take_b(*STAGES[k - 1])
        take_x(*STAGES[k - 1])
        if k == 2:
            attend((0,) + STAGES[0], 0, 8, every)
        if k == 3:
            attend(STAGES[1], 0, 8, every)
            attend(STAGES[2], 0, 6, every)
        if k == 4:
            attend(STAGES[2], 6, 2, every)
            attend(STAGES[3], 0, 6, every)

    wide = lax.broadcasted_iota(jnp.int32, (rows, 2 * KD), 1)
    home = []
    for i in (2, 3):
        attend(STAGES[3], 6, 2, (i,))
        at_rows = pl.ds(i * rows, rows)
        total = jnp.sum(tot[at_rows, :], axis=1, keepdims=True)
        acc[at_rows, :] = jnp.where(wide < VD, acc[at_rows, :], total)
        home.append(copies.start(acc.at[at_rows], part.at[pl.ds((i - 2) * rows, rows)], twin))
    attend(STAGES[3], 6, 2, (0, 1))
    for h in range(HEADS):
        if h % 4 == 0:
            home[h // 4].wait_recv()
        at_rows = pl.ds(h * TOK, TOK)
        both = acc[at_rows, :VD] + part[at_rows, :VD]
        total = jnp.sum(tot[at_rows, :], axis=1, keepdims=True) + part[at_rows, VD : VD + 1]
        out_ref[:, h * VD : (h + 1) * VD] = (both * (1.0 / total)).astype(BF16)
    for copy in copies.made:
        copy.wait_send()
    assert len(copies.made) <= N_COPIES


def tables():
    frequency = np.exp(np.arange(KD // 2) * (-2.0 * math.log(ROPE_BASE) / KD))

    def both(places):
        angles = places[:, None] * frequency[None, :]
        return np.concatenate([np.cos(angles)] * 2 + [np.sin(angles)] * 2, axis=1).astype(np.float32)

    return both(np.arange(TOK)), both(np.arange(2 * NX * NZ) * TOK)


def on_device(
    dna_bases, stem_weight, stem_bias, conv_weight, conv_bias, norm_gain, query_weight, key_weight, value_weight
):
    rope, step = tables()
    vmem = pl.BlockSpec(memory_space=pltpu.VMEM)
    anywhere = pl.BlockSpec(memory_space=pltpu.HBM)
    return pl.pallas_call(
        kernel,
        out_shape=jax.ShapeDtypeStruct((TOK, HEADS * VD), BF16),
        in_specs=[anywhere] * 11,
        out_specs=vmem,
        scratch_shapes=[
            pltpu.VMEM((2, 128), jnp.int32),
            pltpu.VMEM((TAPS, 4, C1), BF16),
            pltpu.VMEM((C1,), F32),
            pltpu.VMEM((C2,), F32),
            pltpu.VMEM((C2,), F32),
            pltpu.VMEM((TOK, 2 * KD), F32),
            pltpu.VMEM((1, 2 * KD), F32),
            pltpu.VMEM((2, 2, 128), jnp.int32),
            pltpu.VMEM((40, 512), F32),
            pltpu.VMEM((40, C1), F32),
            pltpu.VMEM((72, C1), F32),
            pltpu.VMEM((72, C1), F32),
            pltpu.VMEM((2 * TOK, TAPS * C1), BF16),
            pltpu.VMEM((TAPS, C1, C2), BF16),
            pltpu.VMEM((C2, HEADS * KD), BF16),
            pltpu.VMEM((C2, KD), BF16),
            pltpu.VMEM((2 * KD, C2), BF16),
            pltpu.VMEM((16, 8, UROWS, 128), BF16),
            pltpu.VMEM((2 * QROWS, KD), BF16),
            pltpu.VMEM((2 * QROWS, 2 * KD), F32),
            pltpu.VMEM((2 * QROWS, 128), F32),
            pltpu.VMEM((QROWS, 2 * KD), F32),
            pltpu.SemaphoreType.DMA((N_COPIES,)),
            pltpu.SemaphoreType.DMA((N_COPIES,)),
            pltpu.SemaphoreType.DMA((13,)),
        ],
        compiler_params=pltpu.CompilerParams(
            collective_id=0, has_side_effects=True, vmem_limit_bytes=44 << 20
        ),
    )(*(
        pltpu.with_memory_space_constraint(one, pltpu.HBM)
        for one in (
            dna_bases, stem_weight, stem_bias, conv_bias, norm_gain, jnp.asarray(rope), jnp.asarray(step),
            conv_weight, query_weight, key_weight, value_weight.T,
        )
    ))


def solution(mesh):
    placed = (P(("batch", "seq")), P(), P(), P(), P(), P(), P(), P(), P())
    return jax.shard_map(
        on_device, mesh=mesh, in_specs=placed, out_specs=P(("batch", "seq"), None), check_vma=False
    )
```
